32 devices in a mesh: groups: 2 (over y), ctx: 4 (over z), mp: 2 (over x), rep: 2 (over core).
Axes of the slice: x: 2, y: 2, z: 4, core: 2. Of those that a mesh axis runs over, the one named last changes fastest.
Arguments:
- lru_in: bfloat16 [2048, 4096], P(('groups', 'ctx', 'mp'), 'rep'), parts along dimension 0, may hold values from -6 to 6
- gate_weights: bfloat16 [2, 16, 256, 256], P(None, 'rep', 'mp'), may hold values from -0.375 to 0.375
- decay_param: float32 [4096], P('rep'), may hold values from 4 to 13
- queries: bfloat16 [2048, 2048], P(('groups', 'ctx', 'mp'), 'rep'), parts along dimension 0, may hold values from -7.5 to 7.5
- keys_values: bfloat16 [2048, 256], P(('groups', 'ctx', 'mp')), parts along dimension 0, may hold values from -4 to 4
Outputs:
- recurrent: bfloat16 [2048, 4096], P(('groups', 'ctx', 'mp'), 'rep'), parts along dimension 0
- attended: bfloat16 [2048, 2048], P(('groups', 'ctx', 'mp'), 'rep'), parts along dimension 0
The draws below stay inside these ranges and needn't reach their ends.
There are 2 independent parts, one for each index of `groups`. The reference program is written for one: setup_inputs(seed, part) draws one part's arguments, and reference() takes and returns one part's arrays. A program takes and returns all parts, laid end to end along the dimension named above; an argument that names none is the same for every part. Nothing has to cross between parts.
All inputs are finite; a program needn't handle non-finite values.
Results may differ from the reference program's by a relative error of at most 0.0048.
Values may be sent and summed in bfloat16 or wider, within the bound.
A program may use at most 64 MiB of HBM per device.

```python
import math
import jax
import jax.numpy as jnp
from jax import lax

LRU = 4096
BW = 256
H = 16
HD = 128
WINDOW = 2048
NB = 16
SEQ = 1024


def draw_queries(key, part):
    sampled = jax.random.truncated_normal(jax.random.fold_in(key, 1), -4.0, 4.0, (SEQ, H, HD), jnp.float32)
    return sampled.reshape(SEQ, H * HD).astype(jnp.bfloat16)


def draw_keys_values(key, part):
    sampled = jax.random.truncated_normal(jax.random.fold_in(key, 2), -4.0, 4.0, (SEQ, 2 * HD), jnp.float32)
    return sampled.astype(jnp.bfloat16)


def level_of(key, extent, pieces, least, high):
    def one(position, blocks):
        draws = jax.random.uniform(jax.random.fold_in(jax.random.fold_in(key, 6), position), (blocks,), jnp.float32, least / len(pieces), high / len(pieces))
        return jnp.repeat(jnp.exp(draws), extent[position] // blocks).reshape((-1,) + (1,) * (len(extent) - position - 1))

    level = one(*pieces[0])
    for cut in pieces[1:]:
        level = level * one(*cut)
    return level


def bell_draw(rng, extent, spread, most, split=(), held_as=jnp.bfloat16):
    entries = jax.random.normal(rng, extent, jnp.float32) * spread
    if len(split) > 0:
        entries = level_of(rng, extent, split, -0.22, 0.18) * entries
    return jnp.clip(entries, min=-most, max=most).astype(held_as)


def setup_inputs(seed: int = 0, part: int = 0) -> dict:
    key_list = jax.random.split(jax.random.key(seed), 6)
    part_splits = jax.random.split(jax.random.fold_in(key_list[5], part), 6)
    return {
        "lru_in": bell_draw(part_splits[0], (SEQ, LRU), 1.0, 6.0, ((0, 8), (1, 2))),
        "gate_weights": bell_draw(key_list[1], (2, NB, BW, BW), BW ** -0.5, 0.375, ((1, 2), (2, 2))),
        "decay_param": jnp.clip(4.0 + 9.0 * jax.random.uniform(key_list[2], (LRU,), jnp.float32) ** level_of(key_list[2], (LRU,), ((0, 2),), -0.2, 0.2), 4.0, 13.0),
        "queries": draw_queries(jax.random.fold_in(jax.random.fold_in(key_list[5], part), 71), part),
        "keys_values": draw_keys_values(jax.random.fold_in(jax.random.fold_in(key_list[5], part), 71), part),
    }


def reference(lru_in, gate_weights, decay_param, queries, keys_values):
    decay_rate = jax.nn.softplus(-decay_param)
    block_rows = math.gcd(SEQ, 512)
    block_total = SEQ // block_rows
    x_blocks = lru_in.reshape(block_total, block_rows, NB, BW)
    weights_wide = gate_weights.astype(jnp.float32)

    def advance_row(state_now, inputs_now):
        state_next = inputs_now[0] * state_now + inputs_now[1]
        return (state_next, state_next)

    def recur_block(state_now, x_block):
        gate_sums = jnp.einsum('tbi,gbio->gtbo', x_block.astype(jnp.float32), weights_wide)
        gate_sums = gate_sums.reshape(2, block_rows, LRU)
        log_decay = -8.0 * decay_rate[None, :] * jax.nn.sigmoid(gate_sums[0])
        driven = jnp.sqrt(-jnp.expm1(2.0 * log_decay)) * jax.nn.sigmoid(gate_sums[1]) * x_block.reshape(block_rows, LRU).astype(jnp.float32)
        decays = jnp.exp(log_decay)
        state_end, states = lax.scan(advance_row, state_now, (decays, driven))
        return (state_end, states.astype(jnp.bfloat16))
    _, states = lax.scan(recur_block, jnp.zeros((LRU,), jnp.float32), x_blocks)
    recurrent = states.reshape(SEQ, LRU)
    score_scale = 1.0 / math.sqrt(HD)
    padded = jnp.concatenate([jnp.zeros((WINDOW, 2 * HD), jnp.bfloat16), keys_values], axis=0)

    def attend(block_index):
        first_row = (block_index * block_rows).astype(jnp.int32)
        context = lax.dynamic_slice_in_dim(padded, first_row, WINDOW + block_rows, 0).astype(jnp.float32)
        query_block = lax.dynamic_slice_in_dim(queries, first_row, block_rows, 0).reshape(block_rows, H, HD).astype(jnp.float32)
        scores = jnp.einsum('thd,kd->htk', query_block, context[:, :HD]) * score_scale
        query_pos = first_row + jnp.arange(block_rows, dtype=jnp.int32)
        key_pos = first_row - WINDOW + jnp.arange(WINDOW + block_rows, dtype=jnp.int32)
        allowed = (key_pos[None, :] >= 0) & (key_pos[None, :] <= query_pos[:, None]) & (key_pos[None, :] > query_pos[:, None] - WINDOW)
        scores = jnp.where(allowed[None, :, :], scores, jnp.float32(-1e+30))
        row_max = lax.optimization_barrier(jnp.max(scores, axis=2, keepdims=True))
        expd = jnp.exp(scores - row_max)
        probabilities = (expd / lax.optimization_barrier(jnp.sum(expd, axis=2, keepdims=True))).astype(jnp.bfloat16)
        result = jnp.einsum('htk,kd->thd', probabilities.astype(jnp.float32), context[:, HD:])
        return result.astype(jnp.bfloat16).reshape(block_rows, H * HD)
    attended = lax.map(attend, jnp.arange(block_total, dtype=jnp.int32)).reshape(SEQ, H * HD)
    return (recurrent, attended)
```

```python
import functools
import math

import jax
import jax.numpy as jnp
from jax import lax
from jax.experimental import pallas as pl
from jax.experimental.pallas import tpu as pltpu
from jax.sharding import PartitionSpec as P

WINDOW = 2048
MESH = pl.DeviceIdType.MESH
F32 = jnp.float32
BF16 = jnp.bfloat16


def kernel(
    sizes,
    x_hbm, w_hbm, decay_ref, q_hbm, kv_hbm,
    att_ref, decay_run, state_run, entering_ref,
    x_ref, wbuf, q_ref, kvbuf, bias, rate, total, totals_in,
    local_sem, kv_send, kv_recv, w_send, w_recv, f_send, f_recv, t_send, t_recv, r_send, r_recv,
):
    G, C, M, R = sizes
    length = C * M
    rows, width = x_ref.shape
    blocks, bw = wbuf.shape[1], wbuf.shape[4]
    share = blocks // G
    slots = kvbuf.shape[0]
    hd = kvbuf.shape[2] // 2
    heads = q_ref.shape[1] // hd
    g, c, m, r = (lax.axis_index(n) for n in ("groups", "ctx", "mp", "rep"))
    place = c * M + m

    def at(position):
        return (g, position // M, position % M, r)

    loads = [
        pltpu.make_async_copy(kv_hbm, kvbuf.at[0], local_sem.at[0]),
        pltpu.make_async_copy(x_hbm, x_ref, local_sem.at[1]),
        pltpu.make_async_copy(w_hbm, wbuf.at[:, :, m], local_sem.at[2]),
        pltpu.make_async_copy(q_hbm, q_ref, local_sem.at[3]),
    ]
    for load in loads:
        load.start()

    barrier = pltpu.get_barrier_semaphore()

    def greet(d, _):
        pl.semaphore_signal(barrier, inc=1, device_id=at((place + d) % length), device_id_type=MESH)
        return 0

    lax.fori_loop(1, length, greet, 0)
    for d in range(1, G):
        pl.semaphore_signal(barrier, inc=1, device_id=((g + d) % G, c, m, r), device_id_type=MESH)
    for d in range(1, R):
        pl.semaphore_signal(barrier, inc=1, device_id=(g, c, m, (r + d) % R), device_id_type=MESH)
    pl.semaphore_wait(barrier, length - 1 + G - 1 + R - 1)
    part = rows // R
    mine = pl.ds(pl.multiple_of(r * part, part), part)

    def kv_copy(d):
        return pltpu.make_async_remote_copy(
            src_ref=kv_hbm.at[mine], dst_ref=kvbuf.at[d, mine],
            send_sem=kv_send.at[d - 1], recv_sem=kv_recv.at[d - 1],
            device_id=at((place + d) % length), device_id_type=MESH,
        )

    def r_copy(e, d, back=0):
        owner = (r + R - back) % R
        piece = kvbuf.at[d, pl.ds(pl.multiple_of(owner * part, part), part)]
        return pltpu.make_async_remote_copy(
            src_ref=piece, dst_ref=piece,
            send_sem=r_send.at[e - 1, d - 1], recv_sem=r_recv.at[e - 1, d - 1],
            device_id=(g, c, m, (r + e) % R), device_id_type=MESH,
        )

    def w_copy(d, k):
        b = g * share + k
        return pltpu.make_async_remote_copy(
            src_ref=w_hbm.at[:, b], dst_ref=wbuf.at[:, b, m],
            send_sem=w_send.at[d - 1, k], recv_sem=w_recv.at[d - 1, k],
            device_id=(g, c, (m + d) % M, r), device_id_type=MESH,
        )

    def f_copy(e, d, k):
        b = g * share + k
        piece = wbuf.at[:, b, (m + M - d) % M]
        return pltpu.make_async_remote_copy(
            src_ref=piece, dst_ref=piece,
            send_sem=f_send.at[e - 1, d - 1, k], recv_sem=f_recv.at[e - 1, d - 1, k],
            device_id=((g + e) % G, c, m, r), device_id_type=MESH,
        )

    def f_arrival(e, d, k):
        b = ((g + G - e) % G) * share + k
        piece = wbuf.at[:, b, (m + M - d) % M]
        return pltpu.make_async_remote_copy(
            src_ref=piece, dst_ref=piece,
            send_sem=f_send.at[e - 1, d - 1, k], recv_sem=f_recv.at[e - 1, d - 1, k],
            device_id=((g + e) % G, c, m, r), device_id_type=MESH,
        )

    def w_arrival(d, k):
        b = g * share + k
        return pltpu.make_async_remote_copy(
            src_ref=w_hbm.at[:, b], dst_ref=wbuf.at[:, b, (m + M - d) % M],
            send_sem=w_send.at[d - 1, k], recv_sem=w_recv.at[d - 1, k],
            device_id=(g, c, (m + d) % M, r), device_id_type=MESH,
        )

    for d in range(1, M):
        w_copy(d, 0).start()
    for d in range(1, slots):
        kv_copy(d).start()
    for k in range(1, share):
        for d in range(1, M):
            w_copy(d, k).start()

    e = jnp.exp(-decay_ref[...])
    s = e / (2.0 + e)
    s2 = s * s
    rate[...] = -16.0 * s * (1.0 + s2 * (1.0 / 3.0 + s2 * (1.0 / 5.0)))

    row = lax.broadcasted_iota(jnp.int32, (rows, rows), 0)
    col = lax.broadcasted_iota(jnp.int32, (rows, rows), 1)
    for d in range(slots):
        back = row - col + d * rows
        allowed = (back >= 0) & (back < WINDOW) & (place >= d)
        bias[:, d * rows : (d + 1) * rows] = jnp.where(allowed, 0.0, -1e30).astype(F32)

    groups8 = rows // 8
    sub = lax.broadcasted_iota(jnp.int32, (groups8, 8, bw), 1)

    def gates(b):
        lanes = pl.ds(pl.multiple_of(b * bw, bw), bw)
        xb = x_ref[:, lanes]
        g0 = jnp.dot(xb, wbuf[0, b].reshape(bw, bw), preferred_element_type=F32)
        g1 = jnp.dot(xb, wbuf[1, b].reshape(bw, bw), preferred_element_type=F32)
        y = rate[:, lanes] * jax.nn.sigmoid(g0)
        poly = 1.0 + y * (1 / 2 + y * (1 / 6 + y * (1 / 24 + y * (1 / 120 + y * (1 / 720)))))
        u = y * poly
        a = (1.0 + u).reshape(groups8, 8, bw)
        v = jnp.sqrt(-u * (2.0 + u)) * jax.nn.sigmoid(g1) * xb.astype(F32)
        v = v.reshape(groups8, 8, bw)
        for shift in (1, 2, 4):
            keep = sub >= shift
            before_v = jnp.where(keep, pltpu.roll(v, shift, 1), 0.0)
            before_a = jnp.where(keep, pltpu.roll(a, shift, 1), 1.0)
            v = a * before_v + v
            a = a * before_a
        ta, tv = jnp.ones((1, bw), F32), jnp.zeros((1, bw), F32)
        for k in range(groups8):
            here = slice(k * 8, k * 8 + 8)
            vk = a[k] * tv + v[k]
            ak = a[k] * ta
            decay_run[here, lanes] = ak
            state_run[here, lanes] = vk
            ta, tv = ak[7:8], vk[7:8]
        total[0:1, lanes] = ta
        total[1:2, lanes] = tv

    scale = 1.0 / math.sqrt(hd)

    def head(h):
        lanes = pl.ds(pl.multiple_of(h * hd, hd), hd)
        keys = kvbuf[:, :, :hd].reshape(slots * rows, hd)
        values = kvbuf[:, :, hd:].reshape(slots * rows, hd)
        scores = lax.dot_general(
            q_ref[:, lanes], keys, (((1,), (1,)), ((), ())), preferred_element_type=F32
        )
        scores = scores * scale + bias[...]
        top = jnp.max(scores, axis=1, keepdims=True)
        weights = jnp.exp(scores - top)
        norm = jnp.sum(weights, axis=1, keepdims=True)
        out = jnp.dot(weights.astype(BF16), values, preferred_element_type=F32)
        att_ref[:, lanes] = (out / norm).astype(BF16)

    loads[1].wait()
    loads[2].wait()

    def direct(k, _):
        for d in range(1, M):
            w_arrival(d, k).wait_recv()
            for e in range(1, G):
                f_copy(e, d, k).start()
        gates(g * share + k)
        return 0

    lax.fori_loop(0, share // 2, direct, 0)
    for d in range(1, slots):
        kv_copy(d).wait_recv()
        for e in range(1, R):
            r_copy(e, d).start()
    lax.fori_loop(share // 2, share, direct, 0)

    loads[0].wait()
    loads[3].wait()
    for d in range(1, slots):
        for e in range(1, R):
            r_copy(e, d, e).wait_recv()

    stages = share * (G - 1)
    early = min(heads // 2, stages)

    def early_head(h, _):
        head(h)
        return 0

    for e in range(1, G):
        def relayed(k, _, e=e):
            stage = (e - 1) * share + k

            @pl.when(stage < early)
            def _():
                head(stage)

            for d in range(1, M):
                f_arrival(e, d, k).wait_recv()
            gates(((g + G - e) % G) * share + k)
            return 0

        lax.fori_loop(0, share, relayed, 0)

    def t_copy(d):
        return pltpu.make_async_remote_copy(
            src_ref=total, dst_ref=totals_in.at[d - 1],
            send_sem=t_send.at[d - 1], recv_sem=t_recv.at[d - 1],
            device_id=at((place + d) % length), device_id_type=MESH,
        )

    def t_start(d, _):
        t_copy(d).start()
        return 0

    lax.fori_loop(1, length, t_start, 0)
    lax.fori_loop(early, heads, early_head, 0)

    def t_fold(i, entering):
        d = length - 1 - i
        t_copy(d).wait_recv()
        new = totals_in[d - 1, 0:1] * entering + totals_in[d - 1, 1:2]
        return jnp.where(place >= d, new, entering)

    entering_ref[...] = lax.fori_loop(0, length - 1, t_fold, jnp.zeros((1, width), F32))

    for d in range(1, slots):
        kv_copy(d).wait_send()
        for e in range(1, R):
            r_copy(e, d).wait_send()

    def w_sent(k, _):
        for d in range(1, M):
            w_copy(d, k).wait_send()
            for e in range(1, G):
                f_copy(e, d, k).wait_send()
        return 0

    lax.fori_loop(0, share, w_sent, 0)

    def t_sent(d, _):
        t_copy(d).wait_send()
        return 0

    lax.fori_loop(1, length, t_sent, 0)


PIECES = 4


def finish_kernel(att, decay_run, state_run, entering, rec_out, att_out, rec, sem):
    rows = rec.shape[0]
    step = rows // PIECES
    copies = [pltpu.make_async_copy(att, att_out, sem.at[PIECES])]
    copies[0].start()
    for k in range(PIECES):
        here = pl.ds(k * step, step)
        rec[here] = (state_run[here] + decay_run[here] * entering[...]).astype(BF16)
        copies.append(pltpu.make_async_copy(rec.at[here], rec_out.at[here], sem.at[k]))
        copies[-1].start()
    for copy in copies:
        copy.wait()


def on_device(lru_in, gate_weights, decay_param, queries, keys_values):
    G, C, M, R = (lax.axis_size(n) for n in ("groups", "ctx", "mp", "rep"))
    length = C * M
    rows, width = lru_in.shape
    _, blocks, depth, bw = gate_weights.shape
    share = blocks // G
    reach = min(WINDOW // rows, length - 1)
    slots = reach + 1
    dma = pltpu.SemaphoreType.DMA
    anywhere = pl.BlockSpec(memory_space=pltpu.HBM)
    vmem = pl.BlockSpec(memory_space=pltpu.VMEM)
    parts = pl.pallas_call(
        functools.partial(kernel, (G, C, M, R)),
        out_shape=(
            pltpu.VMEM(queries.shape, BF16),
            pltpu.VMEM(lru_in.shape, F32),
            pltpu.VMEM(lru_in.shape, F32),
            pltpu.VMEM((1, width), F32),
        ),
        in_specs=[anywhere, anywhere, vmem, anywhere, anywhere],
        out_specs=(vmem,) * 4,
        scratch_shapes=[
            pltpu.VMEM((rows, width), BF16),
            pltpu.VMEM((2, blocks, M, depth, bw), BF16),
            pltpu.VMEM(queries.shape, BF16),
            pltpu.VMEM((slots,) + keys_values.shape, BF16),
            pltpu.VMEM((rows, slots * rows), F32),
            pltpu.VMEM((1, width), F32),
            pltpu.VMEM((2, width), F32),
            pltpu.VMEM((length - 1, 2, width), F32),
            dma((4,)),
            dma((reach,)),
            dma((reach,)),
            dma((M - 1, share)),
            dma((M - 1, share)),
            dma((G - 1, M - 1, share)),
            dma((G - 1, M - 1, share)),
            dma((length - 1,)),
            dma((length - 1,)),
            dma((R - 1, reach)),
            dma((R - 1, reach)),
        ],
        compiler_params=pltpu.CompilerParams(
            collective_id=0, has_side_effects=True, vmem_limit_bytes=64 * 2**20 - 917504 - 2440000
        ),
    )(lru_in, gate_weights, decay_param.reshape(1, width), queries, keys_values)
    return pl.pallas_call(
        finish_kernel,
        out_shape=(
            jax.ShapeDtypeStruct(lru_in.shape, BF16),
            jax.ShapeDtypeStruct(queries.shape, BF16),
        ),
        in_specs=[vmem] * 4,
        out_specs=(anywhere, anywhere),
        scratch_shapes=[pltpu.VMEM((rows, width), BF16), dma((PIECES + 1,))],
        compiler_params=pltpu.CompilerParams(vmem_limit_bytes=8 * 2**20),
    )(*parts)


def solution(mesh):
    in_specs = (
        P(("groups", "ctx", "mp"), "rep"),
        P(None, "rep", "mp", None),
        P("rep"),
        P(("groups", "ctx", "mp"), "rep"),
        P(("groups", "ctx", "mp"), None),
    )
    out_specs = (P(("groups", "ctx", "mp"), "rep"), P(("groups", "ctx", "mp"), "rep"))
    return jax.shard_map(
        on_device, mesh=mesh, in_specs=in_specs, out_specs=out_specs, check_vma=False
    )
```

```python
import functools
import math

import jax
import jax.numpy as jnp
from jax import lax
from jax.experimental import pallas as pl
from jax.experimental.pallas import tpu as pltpu
from jax.sharding import PartitionSpec as P

WINDOW = 2048
MESH = pl.DeviceIdType.MESH
F32 = jnp.float32
BF16 = jnp.bfloat16


FAR_FIRST = 4
EARLY_FROM = 5


def kernel(
    sizes,
    x_hbm, w_hbm, decay_ref, q_hbm, kv_hbm,
    att_ref, decay_run, state_run, entering_ref,
    x_ref, wbuf, q_ref, kvbuf, bias, rate, total, totals_in,
    local_sem, x_send, x_recv, y_send, y_recv, z_send, z_recv, c_send, c_recv,
    e_send, e_recv, n_send, n_recv, k_send, k_recv, r_send, r_recv, t_send, t_recv, token_sem, far_sem,
):
    C, M = sizes
    length = C * M
    rows, width = x_ref.shape
    blocks, depth, bw = wbuf.shape[1], wbuf.shape[3], wbuf.shape[4]
    reach = kvbuf.shape[0] - 1
    hd = kvbuf.shape[3] // 2
    heads = q_ref.shape[1] // hd
    keys_seen = (reach + 1) * M * rows
    g, c, m, r = (lax.axis_index(n) for n in ("groups", "ctx", "mp", "rep"))
    place = c * M + m
    zb = c % 2
    pair = c + 1 - 2 * zb
    parity = (g + zb) % 2
    corner = 2 * g + zb
    beside_x = lambda d: (g, c, (m + d) % M, r)
    beside_y = (1 - g, c, m, r)
    beside_z = (g, pair, m, r)
    beside_core = (g, c, m, 1 - r)
    below = lambda e: (g, c + e, m, r)

    def at(position):
        return (g, position // M, position % M, r)

    def signal(sem, device):
        pl.semaphore_signal(sem, inc=1, device_id=device, device_id_type=MESH)

    def copy(src, dst, send, recv, device):
        return pltpu.make_async_remote_copy(
            src_ref=src, dst_ref=dst, send_sem=send, recv_sem=recv, device_id=device, device_id_type=MESH
        )

    loads = [
        pltpu.make_async_copy(kv_hbm, kvbuf.at[0, m], local_sem.at[0]),
        pltpu.make_async_copy(x_hbm, x_ref, local_sem.at[1]),
        pltpu.make_async_copy(w_hbm, wbuf.at[:, :, m], local_sem.at[2]),
        pltpu.make_async_copy(q_hbm, q_ref, local_sem.at[3]),
    ]

    barrier = pltpu.get_barrier_semaphore()
    for d in range(1, M):
        signal(barrier, beside_x(d))
    signal(barrier, beside_y)
    signal(barrier, beside_core)

    @pl.when(c > 0)
    def _():
        signal(barrier, below(-1))

    @pl.when(c < C - 1)
    def _():
        signal(barrier, below(1))

    for load in loads:
        load.start()

    def double(par, first, i):
        i = jnp.where(first == 0, i, 5 - i)
        return i % 2, par * 3 + i // 2

    def single(which):
        return which % 2, blocks - 2 + which // 2

    def tile(par, first, which, i):
        return single(which) if i == 0 else double(par, first, i - 1)

    def own(i):
        return tile(parity, g, corner, i)

    def from_y(i):
        return tile(1 - parity, 1 - g, 2 * (1 - g) + zb, i)

    def from_z(i):
        return tile(1 - parity, g, 2 * g + 1 - zb, i)

    def x_copy(d, i, source=0):
        t, b = own(i)
        return copy(w_hbm.at[t, b], wbuf.at[t, b, (m + M - source) % M], x_send.at[d - 1, i], x_recv.at[d - 1, i], beside_x(d))

    def y_copy(d, i, which):
        t, b = which(i)
        piece = wbuf.at[t, b, (m + M - d) % M]
        return copy(piece, piece, y_send.at[d - 1, i], y_recv.at[d - 1, i], beside_y)

    def z_copy(d, i, which):
        t, b = which(i)
        piece = wbuf.at[t, b, (m + M - d) % M]
        return copy(piece, piece, z_send.at[d - 1, i], z_recv.at[d - 1, i], beside_z)

    half = depth // 2
    across = 3 - corner

    def corner_copy(d, over, which):
        t, b = single(which)
        piece = wbuf.at[t, b, (m + M - d) % M, pl.ds(over * half, half)]
        device = beside_z if over else beside_y
        return copy(piece, piece, c_send.at[d - 1, over], c_recv.at[d - 1, over], device)

    def relay(i):
        for d in range(1, M):
            x_copy(d, i, d).wait_recv()
            y_copy(d, i, own).start()
            z_copy(d, i, own).start()

    def arrive(i):
        for d in range(1, M):
            x_copy(d, i, d).wait_recv()

    part = rows // 2
    mine = pl.ds(pl.multiple_of(r * part, part), part)
    other = pl.ds(pl.multiple_of((1 - r) * part, part), part)

    def e_copy(d, source=0):
        return copy(kv_hbm.at[mine], kvbuf.at[0, (m + M - source) % M, mine], e_send.at[d - 1], e_recv.at[d - 1], beside_x(d))

    def n_copy(d):
        piece = (m + d) % M
        src = kvbuf.at[0, piece, mine] if d else kv_hbm.at[mine]
        return copy(src, kvbuf.at[1, piece, mine], n_send.at[d], n_recv.at[d], below(1))

    def k_copy(e):
        return copy(kvbuf.at[0, :, mine], kvbuf.at[e, :, mine], k_send.at[e - 2], k_recv.at[e - 2], below(e))

    def r_copy(i, rows_of):
        piece = kvbuf.at[0, (m + i + 1) % M, rows_of] if i < M - 1 else kvbuf.at[i - M + 2, :, rows_of]
        return copy(piece, piece, r_send.at[i], r_recv.at[i], beside_core)

    for e in range(1, reach + 1):
        @pl.when(c < e)
        def _(e=e):
            kvbuf[e] = jnp.zeros(kvbuf.shape[1:], BF16)

    pl.semaphore_wait(barrier, M + 1 + (c > 0).astype(jnp.int32) + (c < C - 1).astype(jnp.int32))

    for d in range(1, M):
        x_copy(d, 0).start()
    for d in range(1, M):
        e_copy(d).start()
    for i in range(1, 7):
        for d in range(1, M):
            x_copy(d, i).start()

    @pl.when(c < C - 1)
    def _():
        n_copy(0).start()

    @pl.when(c > 0)
    def _():
        pl.semaphore_wait(token_sem, 1)

    @pl.when(c < C - 1)
    def _():
        signal(token_sem, below(1))

    def greet(i, _):
        signal(far_sem, at(i))
        return 0

    lax.fori_loop(0, c * M, greet, 0)

    e = jnp.exp(-decay_ref[...])
    s = e / (2.0 + e)
    s2 = s * s
    rate[...] = -16.0 * s * (1.0 + s2 * (1.0 / 3.0 + s2 * (1.0 / 5.0)))

    row = lax.broadcasted_iota(jnp.int32, (rows, rows), 0)
    col = lax.broadcasted_iota(jnp.int32, (rows, rows), 1)
    for e in range(reach + 1):
        for n in range(M):
            back = row - col + (e * M + m - n) * rows
            allowed = (back >= 0) & (back < WINDOW) & (c >= e)
            first = (e * M + n) * rows
            bias[:, first : first + rows] = jnp.where(allowed, 0.0, -1e30).astype(F32)

    groups8 = rows // 8
    sub = lax.broadcasted_iota(jnp.int32, (groups8, 8, bw), 1)

    def gates(b, slot):
        lanes = pl.ds(pl.multiple_of(b * bw, bw), bw)
        xb = x_ref[:, lanes]
        g0 = jnp.dot(xb, wbuf[0, b].reshape(bw, bw), preferred_element_type=F32)
        g1 = jnp.dot(xb, wbuf[1, b].reshape(bw, bw), preferred_element_type=F32)
        y = rate[:, lanes] * jax.nn.sigmoid(g0)
        poly = 1.0 + y * (1 / 2 + y * (1 / 6 + y * (1 / 24 + y * (1 / 120 + y * (1 / 720)))))
        u = y * poly
        a = (1.0 + u).reshape(groups8, 8, bw)
        v = jnp.sqrt(-u * (2.0 + u)) * jax.nn.sigmoid(g1) * xb.astype(F32)
        v = v.reshape(groups8, 8, bw)
        for shift in (1, 2, 4):
            keep = sub >= shift
            before_v = jnp.where(keep, pltpu.roll(v, shift, 1), 0.0)
            before_a = jnp.where(keep, pltpu.roll(a, shift, 1), 1.0)
            v = a * before_v + v
            a = a * before_a
        ta, tv = jnp.ones((1, bw), F32), jnp.zeros((1, bw), F32)
        for k in range(groups8):
            here = slice(k * 8, k * 8 + 8)
            vk = a[k] * tv + v[k]
            ak = a[k] * ta
            decay_run[here, lanes] = ak
            state_run[here, lanes] = vk
            ta, tv = ak[7:8], vk[7:8]
        total[slot, 0:1] = ta
        total[slot, 1:2] = tv

    scale = 1.0 / math.sqrt(hd)

    def head(h):
        lanes = pl.ds(pl.multiple_of(h * hd, hd), hd)
        keys = kvbuf[:, :, :, :hd].reshape(keys_seen, hd)
        values = kvbuf[:, :, :, hd:].reshape(keys_seen, hd)
        scores = lax.dot_general(
            q_ref[:, lanes], keys, (((1,), (1,)), ((), ())), preferred_element_type=F32
        )
        scores = scores * scale + bias[...]
        top = jnp.max(scores, axis=1, keepdims=True)
        weights = jnp.exp(scores - top)
        norm = jnp.sum(weights, axis=1, keepdims=True)
        out = jnp.dot(weights.astype(BF16), values, preferred_element_type=F32)
        att_ref[:, lanes] = (out / norm).astype(BF16)

    def order(slot):
        ends = jnp.where(g == 0, 0, 2)
        mine0, theirs0 = parity * 3, (1 - parity) * 3
        b = slot
        for k, value in enumerate((
            mine0 + ends, theirs0 + 2 - ends, theirs0 + ends, mine0 + 1, theirs0 + 1, mine0 + 2 - ends
        )):
            b = jnp.where(slot == k, value, b)
        return b

    def slot_of(b, source_c):
        if b >= blocks - 2:
            return b
        par = (g + source_c % 2) % 2
        ends = jnp.where(g == 0, 0, 2)
        idx = b % 3
        if idx == 1:
            return jnp.where(par == b // 3, 3, 4)
        same = idx == ends
        return jnp.where(par == b // 3, jnp.where(same, 0, 5), jnp.where(same, 2, 1))

    def t_copy(d, late):
        span = pl.ds(FAR_FIRST, blocks - FAR_FIRST) if late else pl.ds(0, FAR_FIRST)
        return copy(total.at[span], totals_in.at[d - 1, span], t_send.at[d - 1, late], t_recv.at[d - 1, late], at(place + d))

    def t_start(late):
        def one(d, _):
            t_copy(d, late).start()
            return 0

        lax.fori_loop(1, length - place, one, 0)

    def step(slot, _):
        @pl.when(slot == 0)
        def _():
            relay(0)
            relay(1)

            @pl.when(c < C - 1)
            def _():
                pl.semaphore_wait(far_sem, (C - 1 - c) * M)

            loads[0].wait()
            for d in range(1, M):
                e_copy(d, d).wait_recv()

            @pl.when(c < C - 1)
            def _():
                for d in range(1, M):
                    n_copy(d).start()

            for e in range(2, reach + 1):
                @pl.when(c < C - e)
                def _(e=e):
                    k_copy(e).start()

            for i in range(M - 1):
                r_copy(i, mine).start()
            relay(2)
            loads[1].wait()
            loads[2].wait()

        @pl.when(slot == 1)
        def _():
            for d in range(1, M):
                y_copy(d, 0, from_y).wait_recv()
                corner_copy(d, 1, 2 * (1 - g) + zb).start()
                z_copy(d, 0, from_z).wait_recv()
                corner_copy(d, 0, 2 * g + 1 - zb).start()
            relay(3)
            for d in range(1, M):
                y_copy(d, 1, from_y).wait_recv()
                y_copy(d, 2, from_y).wait_recv()

        @pl.when(slot == 2)
        def _():
            for d in range(1, M):
                z_copy(d, 1, from_z).wait_recv()
                z_copy(d, 2, from_z).wait_recv()

            @pl.when(c > 0)
            def _():
                for d in range(M):
                    n_copy(d).wait_recv()
                r_copy(M - 1, mine).start()

        @pl.when(slot == 3)
        def _():
            arrive(4)
            for e in range(2, reach + 1):
                @pl.when(c >= e)
                def _(e=e):
                    k_copy(e).wait_recv()
                    r_copy(M - 2 + e, mine).start()

        @pl.when(slot == 4)
        def _():
            t_start(0)
            for d in range(1, M):
                y_copy(d, 3, from_y).wait_recv()
                z_copy(d, 3, from_z).wait_recv()

        @pl.when(slot == EARLY_FROM)
        def _():
            for i in range(M - 1):
                r_copy(i, other).wait_recv()
            for e in range(1, reach + 1):
                @pl.when(c >= e)
                def _(e=e):
                    r_copy(M - 2 + e, other).wait_recv()

            loads[3].wait()

        @pl.when(slot >= EARLY_FROM)
        def _():
            head(slot - EARLY_FROM)

        @pl.when(slot == 5)
        def _():
            arrive(5)
            arrive(6)

        @pl.when(slot == 6)
        def _():
            for d in range(1, M):
                corner_copy(d, 0, across).wait_recv()
                corner_copy(d, 1, across).wait_recv()

        gates(order(slot), slot)
        return 0

    lax.fori_loop(0, blocks, step, 0)
    t_start(1)

    def late_head(h, _):
        head(h)
        return 0

    lax.fori_loop(blocks - EARLY_FROM, heads, late_head, 0)

    def t_fold(i, entering):
        d = place - i
        t_copy(d, 0).wait_recv()
        t_copy(d, 1).wait_recv()
        new = []
        for b in range(blocks):
            slot = slot_of(b, i // M)
            new.append(totals_in[d - 1, slot, 0:1] * entering[b] + totals_in[d - 1, slot, 1:2])
        return tuple(new)

    entering = lax.fori_loop(0, place, t_fold, (jnp.zeros((1, bw), F32),) * blocks)
    for b in range(blocks):
        entering_ref[:, b * bw : (b + 1) * bw] = entering[b]

    for d in range(1, M):
        e_copy(d).wait_send()
        for i in range(7):
            x_copy(d, i).wait_send()
        for i in range(4):
            y_copy(d, i, own).wait_send()
            z_copy(d, i, own).wait_send()
        corner_copy(d, 1, 2 * (1 - g) + zb).wait_send()
        corner_copy(d, 0, 2 * g + 1 - zb).wait_send()
    for i in range(M - 1):
        r_copy(i, mine).wait_send()
    for e in range(1, reach + 1):
        @pl.when(c >= e)
        def _(e=e):
            r_copy(M - 2 + e, mine).wait_send()

    @pl.when(c < C - 1)
    def _():
        for d in range(M):
            n_copy(d).wait_send()

    for e in range(2, reach + 1):
        @pl.when(c < C - e)
        def _(e=e):
            k_copy(e).wait_send()

    def t_sent(d, _):
        t_copy(d, 0).wait_send()
        t_copy(d, 1).wait_send()
        return 0

    lax.fori_loop(1, length - place, t_sent, 0)


PIECES = 4


def finish_kernel(att, decay_run, state_run, entering, rec_out, att_out, rec, sem):
    rows = rec.shape[0]
    step = rows // PIECES
    copies = [pltpu.make_async_copy(att, att_out, sem.at[PIECES])]
    copies[0].start()
    for k in range(PIECES):
        here = pl.ds(k * step, step)
        rec[here] = (state_run[here] + decay_run[here] * entering[...]).astype(BF16)
        copies.append(pltpu.make_async_copy(rec.at[here], rec_out.at[here], sem.at[k]))
        copies[-1].start()
    for copy in copies:
        copy.wait()


def on_device(lru_in, gate_weights, decay_param, queries, keys_values):
    G, C, M, R = (lax.axis_size(n) for n in ("groups", "ctx", "mp", "rep"))
    length = C * M
    rows, width = lru_in.shape
    _, blocks, depth, bw = gate_weights.shape
    assert (G, R, C % 2, blocks) == (2, 2, 0, 8)
    reach = min((WINDOW // rows + M - 1) // M, C - 1)
    dma = pltpu.SemaphoreType.DMA
    anywhere = pl.BlockSpec(memory_space=pltpu.HBM)
    vmem = pl.BlockSpec(memory_space=pltpu.VMEM)
    parts = pl.pallas_call(
        functools.partial(kernel, (C, M)),
        out_shape=(
            pltpu.VMEM(queries.shape, BF16),
            pltpu.VMEM(lru_in.shape, F32),
            pltpu.VMEM(lru_in.shape, F32),
            pltpu.VMEM((1, width), F32),
        ),
        in_specs=[anywhere, anywhere, vmem, anywhere, anywhere],
        out_specs=(vmem,) * 4,
        scratch_shapes=[
            pltpu.VMEM((rows, width), BF16),
            pltpu.VMEM((2, blocks, M, depth, bw), BF16),
            pltpu.VMEM(queries.shape, BF16),
            pltpu.VMEM((reach + 1, M) + keys_values.shape, BF16),
            pltpu.VMEM((rows, (reach + 1) * M * rows), F32),
            pltpu.VMEM((1, width), F32),
            pltpu.VMEM((blocks, 2, bw), F32),
            pltpu.VMEM((length - 1, blocks, 2, bw), F32),
            dma((4,)),
            dma((M - 1, 7)),
            dma((M - 1, 7)),
            dma((M - 1, 4)),
            dma((M - 1, 4)),
            dma((M - 1, 4)),
            dma((M - 1, 4)),
            dma((M - 1, 2)),
            dma((M - 1, 2)),
            dma((M - 1,)),
            dma((M - 1,)),
            dma((M,)),
            dma((M,)),
            dma((reach - 1,)),
            dma((reach - 1,)),
            dma((reach + M - 1,)),
            dma((reach + M - 1,)),
            dma((length - 1, 2)),
            dma((length - 1, 2)),
            pltpu.SemaphoreType.REGULAR,
            pltpu.SemaphoreType.REGULAR,
        ],
        compiler_params=pltpu.CompilerParams(
            collective_id=0, has_side_effects=True, vmem_limit_bytes=64 * 2**20 - 917504 - 2440000
        ),
    )(lru_in, gate_weights, decay_param.reshape(1, width), queries, keys_values)
    return pl.pallas_call(
        finish_kernel,
        out_shape=(
            jax.ShapeDtypeStruct(lru_in.shape, BF16),
            jax.ShapeDtypeStruct(queries.shape, BF16),
        ),
        in_specs=[vmem] * 4,
        out_specs=(anywhere, anywhere),
        scratch_shapes=[pltpu.VMEM((rows, width), BF16), dma((PIECES + 1,))],
        compiler_params=pltpu.CompilerParams(vmem_limit_bytes=8 * 2**20),
    )(*parts)


def solution(mesh):
    in_specs = (
        P(("groups", "ctx", "mp"), "rep"),
        P(None, "rep", "mp", None),
        P("rep"),
        P(("groups", "ctx", "mp"), "rep"),
        P(("groups", "ctx", "mp"), None),
    )
    out_specs = (P(("groups", "ctx", "mp"), "rep"), P(("groups", "ctx", "mp"), "rep"))
    return jax.shard_map(
        on_device, mesh=mesh, in_specs=in_specs, out_specs=out_specs, check_vma=False
    )
```

```python
import functools
import math

import jax
import jax.numpy as jnp
from jax import lax
from jax.experimental import pallas as pl
from jax.experimental.pallas import tpu as pltpu
from jax.sharding import PartitionSpec as P

WINDOW = 2048
MESH = pl.DeviceIdType.MESH
F32 = jnp.float32
BF16 = jnp.bfloat16


FAR_FIRST = 4


def kernel(
    sizes,
    x_hbm, w_hbm, decay_hbm, q_hbm, kv_hbm,
    att_ref, decay_run, state_run, entering_ref,
    x_ref, wbuf, q_ref, kvbuf, decay_ref, bias, rate, total, totals_in,
    local_sem, x_send, x_recv, y_send, y_recv, z_send, z_recv, c_send, c_recv,
    e_send, e_recv, k_send, k_recv, r_send, r_recv, t_send, t_recv, far_sem,
):
    C, M = sizes
    length = C * M
    rows, width = x_ref.shape
    blocks, depth, bw = wbuf.shape[1], wbuf.shape[3], wbuf.shape[4]
    reach = kvbuf.shape[0] - 1
    hd = kvbuf.shape[3] // 2
    heads = q_ref.shape[1] // hd
    keys_seen = (reach + 1) * M * rows
    g, c, m, r = (lax.axis_index(n) for n in ("groups", "ctx", "mp", "rep"))
    place = c * M + m
    zb = c % 2
    pair = c + 1 - 2 * zb
    parity = (g + zb) % 2
    corner = 2 * g + zb
    beside_x = lambda d: (g, c, (m + d) % M, r)
    beside_y = (1 - g, c, m, r)
    beside_z = (g, pair, m, r)
    beside_core = (g, c, m, 1 - r)
    below = lambda e: (g, c + e, m, r)

    def at(position):
        return (g, position // M, position % M, r)

    def signal(sem, device):
        pl.semaphore_signal(sem, inc=1, device_id=device, device_id_type=MESH)

    def copy(src, dst, send, recv, device):
        return pltpu.make_async_remote_copy(
            src_ref=src, dst_ref=dst, send_sem=send, recv_sem=recv, device_id=device, device_id_type=MESH
        )

    loads = [
        pltpu.make_async_copy(kv_hbm, kvbuf.at[0, m], local_sem.at[0]),
        pltpu.make_async_copy(x_hbm, x_ref, local_sem.at[1]),
        pltpu.make_async_copy(w_hbm, wbuf.at[:, :, m], local_sem.at[2]),
        pltpu.make_async_copy(q_hbm, q_ref, local_sem.at[3]),
        pltpu.make_async_copy(decay_hbm, decay_ref, local_sem.at[4]),
    ]

    barrier = pltpu.get_barrier_semaphore()
    for d in range(1, M):
        signal(barrier, beside_x(d))
    signal(barrier, beside_y)
    signal(barrier, beside_core)

    @pl.when(c > 0)
    def _():
        signal(barrier, below(-1))

    def greet_later(i, _):
        signal(barrier, at(i))
        return 0

    lax.fori_loop((c + 1) * M, length, greet_later, 0)

    for load in loads:
        load.start()

    def double(par, first, i):
        i = jnp.where(first == 0, i, 5 - i)
        return i % 2, par * 3 + i // 2

    def single(which):
        return which % 2, blocks - 2 + which // 2

    def tile(par, first, which, i):
        return single(which) if i == 0 else double(par, first, i - 1)

    def own(i):
        return tile(parity, g, corner, i)

    def from_y(i):
        return tile(1 - parity, 1 - g, 2 * (1 - g) + zb, i)

    def from_z(i):
        return tile(1 - parity, g, 2 * g + 1 - zb, i)

    def x_copy(d, i, source=0):
        t, b = own(i)
        return copy(w_hbm.at[t, b], wbuf.at[t, b, (m + M - source) % M], x_send.at[d - 1, i], x_recv.at[d - 1, i], beside_x(d))

    def y_copy(d, i, which):
        t, b = which(i)
        piece = wbuf.at[t, b, (m + M - d) % M]
        return copy(piece, piece, y_send.at[d - 1, i], y_recv.at[d - 1, i], beside_y)

    def z_copy(d, i, which):
        t, b = which(i)
        piece = wbuf.at[t, b, (m + M - d) % M]
        return copy(piece, piece, z_send.at[d - 1, i], z_recv.at[d - 1, i], beside_z)

    across = 3 - corner

    def corner_copy(d, which):
        t, b = single(which)
        piece = wbuf.at[t, b, (m + M - d) % M]
        return copy(piece, piece, c_send.at[d - 1], c_recv.at[d - 1], beside_y)

    def relay(i):
        for d in range(1, M):
            x_copy(d, i, d).wait_recv()
            y_copy(d, i, own).start()
            z_copy(d, i, own).start()

    def arrive(i):
        for d in range(1, M):
            x_copy(d, i, d).wait_recv()

    part = rows // 2
    mine = pl.ds(pl.multiple_of(r * part, part), part)
    other = pl.ds(pl.multiple_of((1 - r) * part, part), part)

    def e_copy(d, source=0):
        return copy(kv_hbm.at[mine], kvbuf.at[0, (m + M - source) % M, mine], e_send.at[d - 1], e_recv.at[d - 1], beside_x(d))

    def k_copy(e, d):
        piece = (m + d) % M
        src = kv_hbm.at[mine] if (e, d) == (1, 0) else kvbuf.at[e - 1, piece, mine]
        return copy(src, kvbuf.at[e, piece, mine], k_send.at[e - 1, d], k_recv.at[e - 1, d], below(1))

    def r_copy(i, rows_of):
        piece = kvbuf.at[0, (m + i + 1) % M, rows_of] if i < M - 1 else kvbuf.at[i - M + 2, :, rows_of]
        return copy(piece, piece, r_send.at[i], r_recv.at[i], beside_core)

    for e in range(1, reach + 1):
        @pl.when(c < e)
        def _(e=e):
            kvbuf[e] = jnp.zeros(kvbuf.shape[1:], BF16)

    pl.semaphore_wait(barrier, M + 1 + c * M + (c < C - 1).astype(jnp.int32))

    def greet(i, _):
        signal(far_sem, at(i))
        return 0

    lax.fori_loop(0, c * M, greet, 0)

    for d in range(1, M):
        x_copy(d, 0).start()
    for d in range(1, M):
        e_copy(d).start()
    for i in range(1, 7):
        for d in range(1, M):
            x_copy(d, i).start()

    @pl.when(c < C - 1)
    def _():
        k_copy(1, 0).start()

    loads[4].wait()
    e = jnp.exp(-decay_ref[...])
    s = e / (2.0 + e)
    s2 = s * s
    rate[...] = -16.0 * s * (1.0 + s2 * (1.0 / 3.0 + s2 * (1.0 / 5.0)))

    row = lax.broadcasted_iota(jnp.int32, (rows, rows), 0)
    col = lax.broadcasted_iota(jnp.int32, (rows, rows), 1)
    for e in range(reach + 1):
        for n in range(M):
            back = row - col + (e * M + m - n) * rows
            allowed = (back >= 0) & (back < WINDOW) & (c >= e)
            first = (e * M + n) * rows
            bias[:, first : first + rows] = jnp.where(allowed, 0.0, -1e30).astype(F32)

    groups8 = rows // 8
    sub = lax.broadcasted_iota(jnp.int32, (groups8, 8, bw), 1)

    def gates(b, slot):
        lanes = pl.ds(pl.multiple_of(b * bw, bw), bw)
        xb = x_ref[:, lanes]
        g0 = jnp.dot(xb, wbuf[0, b].reshape(bw, bw), preferred_element_type=F32)
        g1 = jnp.dot(xb, wbuf[1, b].reshape(bw, bw), preferred_element_type=F32)
        y = rate[:, lanes] * jax.nn.sigmoid(g0)
        poly = 1.0 + y * (1 / 2 + y * (1 / 6 + y * (1 / 24 + y * (1 / 120 + y * (1 / 720)))))
        u = y * poly
        a = (1.0 + u).reshape(groups8, 8, bw)
        v = jnp.sqrt(-u * (2.0 + u)) * jax.nn.sigmoid(g1) * xb.astype(F32)
        v = v.reshape(groups8, 8, bw)
        for shift in (1, 2, 4):
            keep = sub >= shift
            before_v = jnp.where(keep, pltpu.roll(v, shift, 1), 0.0)
            before_a = jnp.where(keep, pltpu.roll(a, shift, 1), 1.0)
            v = a * before_v + v
            a = a * before_a
        ta, tv = jnp.ones((1, bw), F32), jnp.zeros((1, bw), F32)
        for k in range(groups8):
            here = slice(k * 8, k * 8 + 8)
            vk = a[k] * tv + v[k]
            ak = a[k] * ta
            decay_run[here, lanes] = ak
            state_run[here, lanes] = vk
            ta, tv = ak[7:8], vk[7:8]
        total[slot, 0:1] = ta
        total[slot, 1:2] = tv

    scale = 1.0 / math.sqrt(hd)

    def head(h):
        lanes = pl.ds(pl.multiple_of(h * hd, hd), hd)
        keys = kvbuf[:, :, :, :hd].reshape(keys_seen, hd)
        values = kvbuf[:, :, :, hd:].reshape(keys_seen, hd)
        scores = lax.dot_general(
            q_ref[:, lanes], keys, (((1,), (1,)), ((), ())), preferred_element_type=F32
        )
        scores = scores * scale + bias[...]
        top = jnp.max(scores, axis=1, keepdims=True)
        weights = jnp.exp(scores - top)
        norm = jnp.sum(weights, axis=1, keepdims=True)
        out = jnp.dot(weights.astype(BF16), values, preferred_element_type=F32)
        att_ref[:, lanes] = (out / norm).astype(BF16)

    def order(slot):
        ends = jnp.where(g == 0, 0, 2)
        mine0, theirs0 = parity * 3, (1 - parity) * 3
        b = slot
        for k, value in enumerate((
            mine0 + ends, theirs0 + 2 - ends, theirs0 + ends, mine0 + 1, theirs0 + 1, mine0 + 2 - ends
        )):
            b = jnp.where(slot == k, value, b)
        return b

    def slot_of(b, source_c):
        if b >= blocks - 2:
            return b
        par = (g + source_c % 2) % 2
        ends = jnp.where(g == 0, 0, 2)
        idx = b % 3
        if idx == 1:
            return jnp.where(par == b // 3, 3, 4)
        same = idx == ends
        return jnp.where(par == b // 3, jnp.where(same, 0, 5), jnp.where(same, 2, 1))

    def t_copy(d, late):
        span = pl.ds(FAR_FIRST, blocks - FAR_FIRST) if late else pl.ds(0, FAR_FIRST)
        return copy(total.at[span], totals_in.at[d - 1, span], t_send.at[d - 1, late], t_recv.at[d - 1, late], at(place + d))

    def t_start(late):
        def one(d, _):
            t_copy(d, late).start()
            return 0

        lax.fori_loop(1, length - place, one, 0)

    def pass_on(e, ds):
        if e > reach:
            return

        @pl.when(c >= e)
        def _():
            for d in ds:
                k_copy(e, d).wait_recv()

            if e < reach:
                @pl.when(c < C - 1)
                def _():
                    for d in ds:
                        k_copy(e + 1, d).start()

            if ds[-1]:
                r_copy(M - 2 + e, mine).start()

    straight, crossed = (0,), tuple(range(1, M))

    def step(slot, _):
        @pl.when(slot == 0)
        def _():
            pass_on(1, straight)
            relay(0)
            loads[0].wait()
            for d in range(1, M):
                e_copy(d, d).wait_recv()

            @pl.when(c < C - 1)
            def _():
                for d in range(1, M):
                    k_copy(1, d).start()

            for i in range(M - 1):
                r_copy(i, mine).start()
            pass_on(2, straight)
            relay(1)
            pass_on(1, crossed)
            relay(2)
            loads[1].wait()
            loads[2].wait()

        @pl.when(slot == 1)
        def _():
            for d in range(1, M):
                z_copy(d, 0, from_z).wait_recv()
                corner_copy(d, 2 * g + 1 - zb).start()
            for e in range(3, reach + 1):
                pass_on(e, straight)
            relay(3)
            pass_on(2, crossed)
            for d in range(1, M):
                y_copy(d, 1, from_y).wait_recv()
                y_copy(d, 2, from_y).wait_recv()

        @pl.when(slot == 2)
        def _():
            for d in range(1, M):
                z_copy(d, 1, from_z).wait_recv()
                z_copy(d, 2, from_z).wait_recv()

        @pl.when(slot == 3)
        def _():
            arrive(4)
            for e in range(3, reach + 1):
                pass_on(e, crossed)

        @pl.when(slot == 4)
        def _():
            @pl.when(c < C - 1)
            def _():
                pl.semaphore_wait(far_sem, (C - 1 - c) * M)

            t_start(0)
            for d in range(1, M):
                y_copy(d, 3, from_y).wait_recv()
                z_copy(d, 3, from_z).wait_recv()

        @pl.when(slot == 5)
        def _():
            arrive(5)
            arrive(6)

        @pl.when(slot == 6)
        def _():
            for d in range(1, M):
                y_copy(d, 0, from_y).wait_recv()
                corner_copy(d, across).wait_recv()

        gates(order(slot), slot)
        return 0

    lax.fori_loop(0, blocks, step, 0)
    t_start(1)

    loads[3].wait()
    for i in range(M - 1):
        r_copy(i, other).wait_recv()
    for e in range(1, reach + 1):
        @pl.when(c >= e)
        def _(e=e):
            r_copy(M - 2 + e, other).wait_recv()

    def late_head(h, _):
        head(h)
        return 0

    lax.fori_loop(0, heads, late_head, 0)

    def t_fold(i, entering):
        d = place - i
        t_copy(d, 0).wait_recv()
        t_copy(d, 1).wait_recv()
        new = []
        for b in range(blocks):
            slot = slot_of(b, i // M)
            new.append(totals_in[d - 1, slot, 0:1] * entering[b] + totals_in[d - 1, slot, 1:2])
        return tuple(new)

    entering = lax.fori_loop(0, place, t_fold, (jnp.zeros((1, bw), F32),) * blocks)
    for b in range(blocks):
        entering_ref[:, b * bw : (b + 1) * bw] = entering[b]

    for d in range(1, M):
        e_copy(d).wait_send()
        for i in range(7):
            x_copy(d, i).wait_send()
        for i in range(4):
            y_copy(d, i, own).wait_send()
            z_copy(d, i, own).wait_send()
        corner_copy(d, 2 * g + 1 - zb).wait_send()
    for i in range(M - 1):
        r_copy(i, mine).wait_send()
    for e in range(1, reach + 1):
        @pl.when(c >= e)
        def _(e=e):
            r_copy(M - 2 + e, mine).wait_send()

    for e in range(1, reach + 1):
        @pl.when((c >= e - 1) & (c < C - 1))
        def _(e=e):
            for d in range(M):
                k_copy(e, d).wait_send()

    def t_sent(d, _):
        t_copy(d, 0).wait_send()
        t_copy(d, 1).wait_send()
        return 0

    lax.fori_loop(1, length - place, t_sent, 0)


PIECES = 4


def finish_kernel(att, decay_run, state_run, entering, rec_out, att_out, rec, sem):
    rows = rec.shape[0]
    step = rows // PIECES
    copies = [pltpu.make_async_copy(att, att_out, sem.at[PIECES])]
    copies[0].start()
    for k in range(PIECES):
        here = pl.ds(k * step, step)
        rec[here] = (state_run[here] + decay_run[here] * entering[...]).astype(BF16)
        copies.append(pltpu.make_async_copy(rec.at[here], rec_out.at[here], sem.at[k]))
        copies[-1].start()
    for copy in copies:
        copy.wait()


def on_device(lru_in, gate_weights, decay_param, queries, keys_values):
    G, C, M, R = (lax.axis_size(n) for n in ("groups", "ctx", "mp", "rep"))
    length = C * M
    rows, width = lru_in.shape
    _, blocks, depth, bw = gate_weights.shape
    assert (G, R, C % 2, blocks) == (2, 2, 0, 8)
    reach = min((WINDOW // rows + M - 1) // M, C - 1)
    dma = pltpu.SemaphoreType.DMA
    anywhere = pl.BlockSpec(memory_space=pltpu.HBM)
    vmem = pl.BlockSpec(memory_space=pltpu.VMEM)
    parts = pl.pallas_call(
        functools.partial(kernel, (C, M)),
        out_shape=(
            pltpu.VMEM(queries.shape, BF16),
            pltpu.VMEM(lru_in.shape, F32),
            pltpu.VMEM(lru_in.shape, F32),
            pltpu.VMEM((1, width), F32),
        ),
        in_specs=[anywhere] * 5,
        out_specs=(vmem,) * 4,
        scratch_shapes=[
            pltpu.VMEM((rows, width), BF16),
            pltpu.VMEM((2, blocks, M, depth, bw), BF16),
            pltpu.VMEM(queries.shape, BF16),
            pltpu.VMEM((reach + 1, M) + keys_values.shape, BF16),
            pltpu.VMEM((1, width), F32),
            pltpu.VMEM((rows, (reach + 1) * M * rows), F32),
            pltpu.VMEM((1, width), F32),
            pltpu.VMEM((blocks, 2, bw), F32),
            pltpu.VMEM((length - 1, blocks, 2, bw), F32),
            dma((5,)),
            dma((M - 1, 7)),
            dma((M - 1, 7)),
            dma((M - 1, 4)),
            dma((M - 1, 4)),
            dma((M - 1, 4)),
            dma((M - 1, 4)),
            dma((M - 1,)),
            dma((M - 1,)),
            dma((M - 1,)),
            dma((M - 1,)),
            dma((reach, M)),
            dma((reach, M)),
            dma((reach + M - 1,)),
            dma((reach + M - 1,)),
            dma((length - 1, 2)),
            dma((length - 1, 2)),
            pltpu.SemaphoreType.REGULAR,
        ],
        compiler_params=pltpu.CompilerParams(
            collective_id=0, has_side_effects=True, vmem_limit_bytes=64 * 2**20 - 917504 - 2440000
        ),
    )(lru_in, gate_weights, decay_param.reshape(1, width), queries, keys_values)
    return pl.pallas_call(
        finish_kernel,
        out_shape=(
            jax.ShapeDtypeStruct(lru_in.shape, BF16),
            jax.ShapeDtypeStruct(queries.shape, BF16),
        ),
        in_specs=[vmem] * 4,
        out_specs=(anywhere, anywhere),
        scratch_shapes=[pltpu.VMEM((rows, width), BF16), dma((PIECES + 1,))],
        compiler_params=pltpu.CompilerParams(vmem_limit_bytes=8 * 2**20),
    )(*parts)


def solution(mesh):
    in_specs = (
        P(("groups", "ctx", "mp"), "rep"),
        P(None, "rep", "mp", None),
        P("rep"),
        P(("groups", "ctx", "mp"), "rep"),
        P(("groups", "ctx", "mp"), None),
    )
    out_specs = (P(("groups", "ctx", "mp"), "rep"), P(("groups", "ctx", "mp"), "rep"))
    return jax.shard_map(
        on_device, mesh=mesh, in_specs=in_specs, out_specs=out_specs, check_vma=False
    )
```

```python
import functools
import math

import jax
import jax.numpy as jnp
from jax import lax
from jax.experimental import pallas as pl
from jax.experimental.pallas import tpu as pltpu
from jax.sharding import PartitionSpec as P

WINDOW = 2048
MESH = pl.DeviceIdType.MESH
F32 = jnp.float32
BF16 = jnp.bfloat16


FAR_FIRST = 4


def kernel(
    sizes,
    x_hbm, w_hbm, decay_hbm, q_hbm, kv_hbm,
    att_ref, decay_run, state_run, entering_ref,
    x_ref, wbuf, q_ref, kvbuf, near_top, near_norm, near_out, decay_ref, bias, rate, total, totals_in,
    local_sem, x_send, x_recv, y_send, y_recv, z_send, z_recv, c_send, c_recv,
    e_send, e_recv, k_send, k_recv, r_send, r_recv, t_send, t_recv, far_sem,
):
    C, M = sizes
    length = C * M
    rows, width = x_ref.shape
    blocks, depth, bw = wbuf.shape[1], wbuf.shape[3], wbuf.shape[4]
    reach = kvbuf.shape[0] - 1
    hd = kvbuf.shape[3] // 2
    heads = q_ref.shape[1] // hd
    g, c, m, r = (lax.axis_index(n) for n in ("groups", "ctx", "mp", "rep"))
    place = c * M + m
    zb = c % 2
    twin = c + 1 - 2 * zb
    parity = (g + zb) % 2
    corner = 2 * g + zb
    beside_x = lambda d: (g, c, (m + d) % M, r)
    beside_y = (1 - g, c, m, r)
    beside_z = (g, twin, m, r)
    beside_core = (g, c, m, 1 - r)
    below = lambda e: (g, c + e, m, r)

    def at(position):
        return (g, position // M, position % M, r)

    def signal(sem, device):
        pl.semaphore_signal(sem, inc=1, device_id=device, device_id_type=MESH)

    def copy(src, dst, send, recv, device):
        return pltpu.make_async_remote_copy(
            src_ref=src, dst_ref=dst, send_sem=send, recv_sem=recv, device_id=device, device_id_type=MESH
        )

    loads = [
        pltpu.make_async_copy(kv_hbm, kvbuf.at[0, m], local_sem.at[0]),
        pltpu.make_async_copy(x_hbm, x_ref, local_sem.at[1]),
        pltpu.make_async_copy(w_hbm, wbuf.at[:, :, m], local_sem.at[2]),
        pltpu.make_async_copy(q_hbm, q_ref, local_sem.at[3]),
        pltpu.make_async_copy(decay_hbm, decay_ref, local_sem.at[4]),
    ]

    barrier = pltpu.get_barrier_semaphore()
    for d in range(1, M):
        signal(barrier, beside_x(d))
    signal(barrier, beside_y)
    signal(barrier, beside_core)

    @pl.when(c > 0)
    def _():
        signal(barrier, below(-1))

    def greet_later(i, _):
        signal(barrier, at(i))
        return 0

    lax.fori_loop((c + 1) * M, length, greet_later, 0)

    for load in loads:
        load.start()

    def double(par, first, i):
        i = jnp.where(first == 0, i, 5 - i)
        return i % 2, par * 3 + i // 2

    def single(which):
        return which % 2, blocks - 2 + which // 2

    def tile(par, first, which, i):
        return single(which) if i == 0 else double(par, first, i - 1)

    def own(i):
        return tile(parity, g, corner, i)

    def from_y(i):
        return tile(1 - parity, 1 - g, 2 * (1 - g) + zb, i)

    def from_z(i):
        return tile(1 - parity, g, 2 * g + 1 - zb, i)

    def x_copy(d, i, source=0):
        t, b = own(i)
        return copy(w_hbm.at[t, b], wbuf.at[t, b, (m + M - source) % M], x_send.at[d - 1, i], x_recv.at[d - 1, i], beside_x(d))

    def y_copy(d, i, which):
        t, b = which(i)
        piece = wbuf.at[t, b, (m + M - d) % M]
        return copy(piece, piece, y_send.at[d - 1, i], y_recv.at[d - 1, i], beside_y)

    def z_copy(d, i, which):
        t, b = which(i)
        piece = wbuf.at[t, b, (m + M - d) % M]
        return copy(piece, piece, z_send.at[d - 1, i], z_recv.at[d - 1, i], beside_z)

    across = 3 - corner

    def corner_copy(d, which):
        t, b = single(which)
        piece = wbuf.at[t, b, (m + M - d) % M]
        return copy(piece, piece, c_send.at[d - 1], c_recv.at[d - 1], beside_y)

    def relay(i):
        for d in range(1, M):
            x_copy(d, i, d).wait_recv()
            y_copy(d, i, own).start()
            z_copy(d, i, own).start()

    def arrive(i):
        for d in range(1, M):
            x_copy(d, i, d).wait_recv()

    part = rows // 2
    mine = pl.ds(pl.multiple_of(r * part, part), part)
    other = pl.ds(pl.multiple_of((1 - r) * part, part), part)

    def e_copy(d, source=0):
        return copy(kv_hbm.at[mine], kvbuf.at[0, (m + M - source) % M, mine], e_send.at[d - 1], e_recv.at[d - 1], beside_x(d))

    def k_copy(e, d):
        piece = (m + d) % M
        src = kv_hbm.at[mine] if (e, d) == (1, 0) else kvbuf.at[e - 1, piece, mine]
        return copy(src, kvbuf.at[e, piece, mine], k_send.at[e - 1, d], k_recv.at[e - 1, d], below(1))

    def r_copy(i, rows_of):
        piece = kvbuf.at[0, (m + i + 1) % M, rows_of] if i < M - 1 else kvbuf.at[i - M + 2, :, rows_of]
        return copy(piece, piece, r_send.at[i], r_recv.at[i], beside_core)

    for e in range(1, reach + 1):
        @pl.when(c < e)
        def _(e=e):
            kvbuf[e] = jnp.zeros(kvbuf.shape[1:], BF16)

    pl.semaphore_wait(barrier, M + 1 + c * M + (c < C - 1).astype(jnp.int32))

    def greet(i, _):
        signal(far_sem, at(i))
        return 0

    lax.fori_loop(0, c * M, greet, 0)

    for d in range(1, M):
        x_copy(d, 0).start()
    for d in range(1, M):
        e_copy(d).start()
    for i in range(1, 7):
        for d in range(1, M):
            x_copy(d, i).start()

    @pl.when(c < C - 1)
    def _():
        k_copy(1, 0).start()

    loads[4].wait()
    e = jnp.exp(-decay_ref[...])
    s = e / (2.0 + e)
    s2 = s * s
    rate[...] = -16.0 * s * (1.0 + s2 * (1.0 / 3.0 + s2 * (1.0 / 5.0)))

    row = lax.broadcasted_iota(jnp.int32, (rows, rows), 0)
    col = lax.broadcasted_iota(jnp.int32, (rows, rows), 1)
    for e in range(reach + 1):
        for n in range(M):
            back = row - col + (e * M + m - n) * rows
            allowed = (back >= 0) & (back < WINDOW) & (c >= e)
            first = (e * M + n) * rows
            bias[:, first : first + rows] = jnp.where(allowed, 0.0, -1e30).astype(F32)

    groups8 = rows // 8
    sub = lax.broadcasted_iota(jnp.int32, (groups8, 8, bw), 1)

    def gates(b, slot):
        lanes = pl.ds(pl.multiple_of(b * bw, bw), bw)
        xb = x_ref[:, lanes]
        g0 = jnp.dot(xb, wbuf[0, b].reshape(bw, bw), preferred_element_type=F32)
        g1 = jnp.dot(xb, wbuf[1, b].reshape(bw, bw), preferred_element_type=F32)
        y = rate[:, lanes] * jax.nn.sigmoid(g0)
        poly = 1.0 + y * (1 / 2 + y * (1 / 6 + y * (1 / 24 + y * (1 / 120 + y * (1 / 720)))))
        u = y * poly
        a = (1.0 + u).reshape(groups8, 8, bw)
        v = jnp.sqrt(-u * (2.0 + u)) * jax.nn.sigmoid(g1) * xb.astype(F32)
        v = v.reshape(groups8, 8, bw)
        for shift in (1, 2, 4):
            keep = sub >= shift
            before_v = jnp.where(keep, pltpu.roll(v, shift, 1), 0.0)
            before_a = jnp.where(keep, pltpu.roll(a, shift, 1), 1.0)
            v = a * before_v + v
            a = a * before_a
        ta, tv = jnp.ones((1, bw), F32), jnp.zeros((1, bw), F32)
        for k in range(groups8):
            here = slice(k * 8, k * 8 + 8)
            vk = a[k] * tv + v[k]
            ak = a[k] * ta
            decay_run[here, lanes] = ak
            state_run[here, lanes] = vk
            ta, tv = ak[7:8], vk[7:8]
        total[slot, 0:1] = ta
        total[slot, 1:2] = tv

    scale = math.log2(math.e) / math.sqrt(hd)

    def scored(first, last):
        count = (last - first) * M * rows
        q = jnp.concatenate([q_ref[:, h * hd : (h + 1) * hd] for h in range(heads)], axis=0)
        keys = kvbuf[first:last, :, :, :hd].reshape(count, hd)
        scores = lax.dot_general(q, keys, (((1,), (1,)), ((), ())), preferred_element_type=F32)
        scores = scores.reshape(heads, rows, count) * scale + bias[:, first * M * rows : last * M * rows]
        return scores.reshape(heads * rows, count)

    def weighed(weights, first, last):
        values = kvbuf[first:last, :, :, hd:].reshape((last - first) * M * rows, hd)
        return jnp.dot(weights.astype(BF16), values, preferred_element_type=F32)

    def near():
        scores = scored(0, 2)
        top = jnp.max(scores, axis=1, keepdims=True)
        weights = jnp.exp2(scores - top)
        near_top[...] = jnp.broadcast_to(top, near_top.shape)
        near_norm[...] = jnp.broadcast_to(jnp.sum(weights, axis=1, keepdims=True), near_norm.shape)
        near_out[...] = weighed(weights, 0, 2)

    def store(out):
        for h in range(heads):
            att_ref[:, h * hd : (h + 1) * hd] = out[h * rows : (h + 1) * rows].astype(BF16)

    def far():
        scores = scored(2, reach + 1)
        top = jnp.max(scores, axis=1, keepdims=True)
        weights = jnp.exp2(scores - top)
        norm = jnp.broadcast_to(jnp.sum(weights, axis=1, keepdims=True), near_norm.shape)
        top = jnp.broadcast_to(top, near_top.shape)
        both = jnp.maximum(top, near_top[...])
        keep, keep_near = jnp.exp2(top - both), jnp.exp2(near_top[...] - both)
        norm = norm * keep + near_norm[...] * keep_near
        store((weighed(weights, 2, reach + 1) * keep + near_out[...] * keep_near) / norm)

    ends = jnp.where(g == 0, 0, 2)

    def order(slot):
        mine0, theirs0 = parity * 3, (1 - parity) * 3
        b = blocks - 1 - g
        for k, value in enumerate((
            mine0 + ends, blocks - 2 + g, mine0 + 1, theirs0 + 2 - ends, theirs0 + ends, theirs0 + 1, mine0 + 2 - ends
        )):
            b = jnp.where(slot == k, value, b)
        return b

    def slot_of(b, source_c):
        if b >= blocks - 2:
            return jnp.where(b == blocks - 2 + g, 1, 7)
        par = (g + source_c % 2) % 2
        idx = b % 3
        if idx == 1:
            return jnp.where(par == b // 3, 2, 5)
        same = idx == ends
        return jnp.where(par == b // 3, jnp.where(same, 0, 6), jnp.where(same, 4, 3))

    def t_copy(d, late):
        span = pl.ds(FAR_FIRST, blocks - FAR_FIRST) if late else pl.ds(0, FAR_FIRST)
        return copy(total.at[span], totals_in.at[d - 1, span], t_send.at[d - 1, late], t_recv.at[d - 1, late], at(place + d))

    def t_start(late):
        def one(d, _):
            t_copy(d, late).start()
            return 0

        lax.fori_loop(1, length - place, one, 0)

    def pass_on(e, ds):
        if e > reach:
            return

        @pl.when(c >= e)
        def _():
            for d in ds:
                k_copy(e, d).wait_recv()

            if e < reach:
                @pl.when(c < C - 1)
                def _():
                    for d in ds:
                        k_copy(e + 1, d).start()

            if ds[-1]:
                r_copy(M - 2 + e, mine).start()

    straight, crossed = (0,), tuple(range(1, M))

    def step(pair, _):
        @pl.when(pair == 0)
        def _():
            pass_on(1, straight)
            relay(0)
            loads[0].wait()
            for d in range(1, M):
                e_copy(d, d).wait_recv()

            @pl.when(c < C - 1)
            def _():
                for d in range(1, M):
                    k_copy(1, d).start()

            for i in range(M - 1):
                r_copy(i, mine).start()
            pass_on(2, straight)
            relay(1)
            pass_on(1, crossed)
            relay(2)
            for d in range(1, M):
                z_copy(d, 0, from_z).wait_recv()
                corner_copy(d, 2 * g + 1 - zb).start()
            loads[1].wait()
            loads[2].wait()

        @pl.when(pair == 1)
        def _():
            for e in range(3, reach + 1):
                pass_on(e, straight)
            relay(3)
            loads[3].wait()
            for i in range(M - 1):
                r_copy(i, other).wait_recv()

            @pl.when(c >= 1)
            def _():
                r_copy(M - 1, other).wait_recv()

            near()
            pass_on(2, crossed)
            arrive(4)
            for d in range(1, M):
                y_copy(d, 1, from_y).wait_recv()
                y_copy(d, 2, from_y).wait_recv()

        @pl.when(pair == 2)
        def _():
            for d in range(1, M):
                z_copy(d, 1, from_z).wait_recv()
                z_copy(d, 2, from_z).wait_recv()
            for e in range(3, reach + 1):
                pass_on(e, crossed)
            for d in range(1, M):
                y_copy(d, 3, from_y).wait_recv()
                z_copy(d, 3, from_z).wait_recv()

        @pl.when(pair == 3)
        def _():
            @pl.when(c < C - 1)
            def _():
                pl.semaphore_wait(far_sem, (C - 1 - c) * M)

            t_start(0)
            arrive(5)
            arrive(6)
            for d in range(1, M):
                y_copy(d, 0, from_y).wait_recv()
                corner_copy(d, across).wait_recv()

        for slot in (2 * pair, 2 * pair + 1):
            gates(order(slot), slot)
        return 0

    lax.fori_loop(0, blocks // 2, step, 0)
    t_start(1)

    for e in range(2, reach + 1):
        @pl.when(c >= e)
        def _(e=e):
            r_copy(M - 2 + e, other).wait_recv()

    @pl.when(c < 2)
    def _():
        store(near_out[...] / near_norm[...])

    @pl.when(c >= 2)
    def _():
        far()

    def t_fold(i, entering):
        d = place - i
        t_copy(d, 0).wait_recv()
        t_copy(d, 1).wait_recv()
        new = []
        for b in range(blocks):
            slot = slot_of(b, i // M)
            new.append(totals_in[d - 1, slot, 0:1] * entering[b] + totals_in[d - 1, slot, 1:2])
        return tuple(new)

    entering = lax.fori_loop(0, place, t_fold, (jnp.zeros((1, bw), F32),) * blocks)
    for b in range(blocks):
        entering_ref[:, b * bw : (b + 1) * bw] = entering[b]

    for d in range(1, M):
        e_copy(d).wait_send()
        for i in range(7):
            x_copy(d, i).wait_send()
        for i in range(4):
            y_copy(d, i, own).wait_send()
            z_copy(d, i, own).wait_send()
        corner_copy(d, 2 * g + 1 - zb).wait_send()
    for i in range(M - 1):
        r_copy(i, mine).wait_send()
    for e in range(1, reach + 1):
        @pl.when(c >= e)
        def _(e=e):
            r_copy(M - 2 + e, mine).wait_send()

    for e in range(1, reach + 1):
        @pl.when((c >= e - 1) & (c < C - 1))
        def _(e=e):
            for d in range(M):
                k_copy(e, d).wait_send()

    def t_sent(d, _):
        t_copy(d, 0).wait_send()
        t_copy(d, 1).wait_send()
        return 0

    lax.fori_loop(1, length - place, t_sent, 0)


PIECES = 4


def finish_kernel(att, decay_run, state_run, entering, rec_out, att_out, rec, sem):
    rows = rec.shape[0]
    step = rows // PIECES
    copies = [pltpu.make_async_copy(att, att_out, sem.at[PIECES])]
    copies[0].start()
    for k in range(PIECES):
        here = pl.ds(k * step, step)
        rec[here] = (state_run[here] + decay_run[here] * entering[...]).astype(BF16)
        copies.append(pltpu.make_async_copy(rec.at[here], rec_out.at[here], sem.at[k]))
        copies[-1].start()
    for copy in copies:
        copy.wait()


def on_device(lru_in, gate_weights, decay_param, queries, keys_values):
    G, C, M, R = (lax.axis_size(n) for n in ("groups", "ctx", "mp", "rep"))
    length = C * M
    rows, width = lru_in.shape
    _, blocks, depth, bw = gate_weights.shape
    assert (G, R, C % 2, blocks) == (2, 2, 0, 8)
    reach = min((WINDOW // rows + M - 1) // M, C - 1)
    hd = keys_values.shape[1] // 2
    stacked = rows * (queries.shape[1] // hd)
    dma = pltpu.SemaphoreType.DMA
    anywhere = pl.BlockSpec(memory_space=pltpu.HBM)
    vmem = pl.BlockSpec(memory_space=pltpu.VMEM)
    parts = pl.pallas_call(
        functools.partial(kernel, (C, M)),
        out_shape=(
            pltpu.VMEM(queries.shape, BF16),
            pltpu.VMEM(lru_in.shape, F32),
            pltpu.VMEM(lru_in.shape, F32),
            pltpu.VMEM((1, width), F32),
        ),
        in_specs=[anywhere] * 5,
        out_specs=(vmem,) * 4,
        scratch_shapes=[
            pltpu.VMEM((rows, width), BF16),
            pltpu.VMEM((2, blocks, M, depth, bw), BF16),
            pltpu.VMEM(queries.shape, BF16),
            pltpu.VMEM((reach + 1, M) + keys_values.shape, BF16),
            pltpu.VMEM((stacked, hd), F32),
            pltpu.VMEM((stacked, hd), F32),
            pltpu.VMEM((stacked, hd), F32),
            pltpu.VMEM((1, width), F32),
            pltpu.VMEM((rows, (reach + 1) * M * rows), F32),
            pltpu.VMEM((1, width), F32),
            pltpu.VMEM((blocks, 2, bw), F32),
            pltpu.VMEM((length - 1, blocks, 2, bw), F32),
            dma((5,)),
            dma((M - 1, 7)),
            dma((M - 1, 7)),
            dma((M - 1, 4)),
            dma((M - 1, 4)),
            dma((M - 1, 4)),
            dma((M - 1, 4)),
            dma((M - 1,)),
            dma((M - 1,)),
            dma((M - 1,)),
            dma((M - 1,)),
            dma((reach, M)),
            dma((reach, M)),
            dma((reach + M - 1,)),
            dma((reach + M - 1,)),
            dma((length - 1, 2)),
            dma((length - 1, 2)),
            pltpu.SemaphoreType.REGULAR,
        ],
        compiler_params=pltpu.CompilerParams(
            collective_id=0, has_side_effects=True, vmem_limit_bytes=64 * 2**20 - 917504 - 2440000
        ),
    )(lru_in, gate_weights, decay_param.reshape(1, width), queries, keys_values)
    return pl.pallas_call(
        finish_kernel,
        out_shape=(
            jax.ShapeDtypeStruct(lru_in.shape, BF16),
            jax.ShapeDtypeStruct(queries.shape, BF16),
        ),
        in_specs=[vmem] * 4,
        out_specs=(anywhere, anywhere),
        scratch_shapes=[pltpu.VMEM((rows, width), BF16), dma((PIECES + 1,))],
        compiler_params=pltpu.CompilerParams(vmem_limit_bytes=8 * 2**20),
    )(*parts)


def solution(mesh):
    in_specs = (
        P(("groups", "ctx", "mp"), "rep"),
        P(None, "rep", "mp", None),
        P("rep"),
        P(("groups", "ctx", "mp"), "rep"),
        P(("groups", "ctx", "mp"), None),
    )
    out_specs = (P(("groups", "ctx", "mp"), "rep"), P(("groups", "ctx", "mp"), "rep"))
    return jax.shard_map(
        on_device, mesh=mesh, in_specs=in_specs, out_specs=out_specs, check_vma=False
    )
```

```python
import functools
import math

import jax
import jax.numpy as jnp
from jax import lax
from jax.experimental import pallas as pl
from jax.experimental.pallas import tpu as pltpu
from jax.sharding import PartitionSpec as P

WINDOW = 2048
MESH = pl.DeviceIdType.MESH
F32 = jnp.float32
BF16 = jnp.bfloat16


EARLY_PAIRS = 3


def kernel(
    sizes,
    x_hbm, w_hbm, decay_hbm, q_hbm, kv_hbm,
    att_ref, decay_run, state_run, entering_ref,
    x_ref, wbuf, q_ref, kvbuf, near_top, near_norm, near_out, decay_ref, bias, rate, total, totals_in,
    local_sem, x_send, x_recv, y_send, y_recv, z_send, z_recv, c_send, c_recv,
    e_send, e_recv, k_send, k_recv, r_send, r_recv, t_send, t_recv, far_sem,
):
    C, M = sizes
    length = C * M
    rows, width = x_ref.shape
    blocks, depth, bw = wbuf.shape[1], wbuf.shape[3], wbuf.shape[4]
    reach = kvbuf.shape[0] - 1
    hd = kvbuf.shape[3] // 2
    heads = q_ref.shape[1] // hd
    g, c, m, r = (lax.axis_index(n) for n in ("groups", "ctx", "mp", "rep"))
    place = c * M + m
    zb = c % 2
    twin = c + 1 - 2 * zb
    parity = (g + zb) % 2
    corner = 2 * g + zb
    beside_x = lambda d: (g, c, (m + d) % M, r)
    beside_y = (1 - g, c, m, r)
    beside_z = (g, twin, m, r)
    beside_core = (g, c, m, 1 - r)
    below = lambda e: (g, c + e, m, r)

    def at(position):
        return (g, position // M, position % M, r)

    def signal(sem, device):
        pl.semaphore_signal(sem, inc=1, device_id=device, device_id_type=MESH)

    def copy(src, dst, send, recv, device):
        return pltpu.make_async_remote_copy(
            src_ref=src, dst_ref=dst, send_sem=send, recv_sem=recv, device_id=device, device_id_type=MESH
        )

    loads = [
        pltpu.make_async_copy(kv_hbm, kvbuf.at[0, m], local_sem.at[0]),
        pltpu.make_async_copy(x_hbm, x_ref, local_sem.at[1]),
        pltpu.make_async_copy(w_hbm, wbuf.at[:, :, m], local_sem.at[2]),
        pltpu.make_async_copy(q_hbm, q_ref, local_sem.at[3]),
        pltpu.make_async_copy(decay_hbm, decay_ref, local_sem.at[4]),
    ]

    barrier = pltpu.get_barrier_semaphore()
    for d in range(1, M):
        signal(barrier, beside_x(d))
    signal(barrier, beside_y)
    signal(barrier, beside_core)

    @pl.when(c > 0)
    def _():
        signal(barrier, below(-1))

    def greet_later(i, _):
        signal(barrier, at(i))
        return 0

    lax.fori_loop((c + 1) * M, length, greet_later, 0)

    for load in loads:
        load.start()

    def double(par, first, i):
        i = jnp.where(first == 0, i, 5 - i)
        return i % 2, par * 3 + i // 2

    def single(which):
        return which % 2, blocks - 2 + which // 2

    def tile(par, first, which, i):
        return single(which) if i == 0 else double(par, first, i - 1)

    def own(i):
        return tile(parity, g, corner, i)

    def from_y(i):
        return tile(1 - parity, 1 - g, 2 * (1 - g) + zb, i)

    def from_z(i):
        return tile(1 - parity, g, 2 * g + 1 - zb, i)

    def x_copy(d, i, source=0):
        t, b = own(i)
        return copy(w_hbm.at[t, b], wbuf.at[t, b, (m + M - source) % M], x_send.at[d - 1, i], x_recv.at[d - 1, i], beside_x(d))

    def y_copy(d, i, which):
        t, b = which(i)
        piece = wbuf.at[t, b, (m + M - d) % M]
        return copy(piece, piece, y_send.at[d - 1, i], y_recv.at[d - 1, i], beside_y)

    def z_copy(d, i, which):
        t, b = which(i)
        piece = wbuf.at[t, b, (m + M - d) % M]
        return copy(piece, piece, z_send.at[d - 1, i], z_recv.at[d - 1, i], beside_z)

    across = 3 - corner

    def corner_copy(d, which):
        t, b = single(which)
        piece = wbuf.at[t, b, (m + M - d) % M]
        return copy(piece, piece, c_send.at[d - 1], c_recv.at[d - 1], beside_y)

    def relay(i):
        for d in range(1, M):
            x_copy(d, i, d).wait_recv()
            y_copy(d, i, own).start()
            z_copy(d, i, own).start()

    def arrive(i):
        for d in range(1, M):
            x_copy(d, i, d).wait_recv()

    part = rows // 2
    mine = pl.ds(pl.multiple_of(r * part, part), part)
    other = pl.ds(pl.multiple_of((1 - r) * part, part), part)

    def e_copy(d, source=0):
        return copy(kv_hbm.at[mine], kvbuf.at[0, (m + M - source) % M, mine], e_send.at[d - 1], e_recv.at[d - 1], beside_x(d))

    def k_copy(e, d):
        piece = (m + d) % M
        src = kv_hbm.at[mine] if (e, d) == (1, 0) else kvbuf.at[e - 1, piece, mine]
        return copy(src, kvbuf.at[e, piece, mine], k_send.at[e - 1, d], k_recv.at[e - 1, d], below(1))

    def r_copy(i, rows_of):
        piece = kvbuf.at[0, (m + i + 1) % M, rows_of] if i < M - 1 else kvbuf.at[i - M + 2, :, rows_of]
        return copy(piece, piece, r_send.at[i], r_recv.at[i], beside_core)

    pl.semaphore_wait(barrier, M + 1 + c * M + (c < C - 1).astype(jnp.int32))

    for d in range(1, M):
        x_copy(d, 0).start()
    for d in range(1, M):
        e_copy(d).start()
    for i in range(1, 7):
        for d in range(1, M):
            x_copy(d, i).start()

    @pl.when(c < C - 1)
    def _():
        k_copy(1, 0).start()

    def greet(i, _):
        signal(far_sem, at(i))
        return 0

    lax.fori_loop(0, c * M, greet, 0)

    for e in range(1, reach + 1):
        @pl.when(c < e)
        def _(e=e):
            kvbuf[e] = jnp.zeros(kvbuf.shape[1:], BF16)


    loads[4].wait()
    e = jnp.exp(-decay_ref[...])
    s = e / (2.0 + e)
    s2 = s * s
    rate[...] = -16.0 * s * (1.0 + s2 * (1.0 / 3.0 + s2 * (1.0 / 5.0)))

    row = lax.broadcasted_iota(jnp.int32, (rows, rows), 0)
    col = lax.broadcasted_iota(jnp.int32, (rows, rows), 1)
    for e in range(reach + 1):
        for n in range(M):
            back = row - col + (e * M + m - n) * rows
            allowed = (back >= 0) & (back < WINDOW) & (c >= e)
            first = (e * M + n) * rows
            bias[:, first : first + rows] = jnp.where(allowed, 0.0, -1e30).astype(F32)

    groups8 = rows // 8
    sub = lax.broadcasted_iota(jnp.int32, (groups8, 8, bw), 1)

    def gates(b):
        lanes = pl.ds(pl.multiple_of(b * bw, bw), bw)
        xb = x_ref[:, lanes]
        g0 = jnp.dot(xb, wbuf[0, b].reshape(bw, bw), preferred_element_type=F32)
        g1 = jnp.dot(xb, wbuf[1, b].reshape(bw, bw), preferred_element_type=F32)
        y = rate[:, lanes] * jax.nn.sigmoid(g0)
        poly = 1.0 + y * (1 / 2 + y * (1 / 6 + y * (1 / 24 + y * (1 / 120 + y * (1 / 720)))))
        u = y * poly
        a = (1.0 + u).reshape(groups8, 8, bw)
        v = jnp.sqrt(-u * (2.0 + u)) * jax.nn.sigmoid(g1) * xb.astype(F32)
        v = v.reshape(groups8, 8, bw)
        for shift in (1, 2, 4):
            keep = sub >= shift
            before_v = jnp.where(keep, pltpu.roll(v, shift, 1), 0.0)
            before_a = jnp.where(keep, pltpu.roll(a, shift, 1), 1.0)
            v = a * before_v + v
            a = a * before_a
        ta, tv = jnp.ones((1, bw), F32), jnp.zeros((1, bw), F32)
        for k in range(groups8):
            here = slice(k * 8, k * 8 + 8)
            vk = a[k] * tv + v[k]
            ak = a[k] * ta
            decay_run[here, lanes] = ak
            state_run[here, lanes] = vk
            ta, tv = ak[7:8], vk[7:8]
        return ta, tv

    scale = math.log2(math.e) / math.sqrt(hd)

    def scored(first, last):
        count = (last - first) * M * rows
        q = jnp.concatenate([q_ref[:, h * hd : (h + 1) * hd] for h in range(heads)], axis=0)
        keys = kvbuf[first:last, :, :, :hd].reshape(count, hd)
        scores = lax.dot_general(q, keys, (((1,), (1,)), ((), ())), preferred_element_type=F32)
        scores = scores.reshape(heads, rows, count) * scale + bias[:, first * M * rows : last * M * rows]
        return scores.reshape(heads * rows, count)

    def weighed(weights, first, last):
        values = kvbuf[first:last, :, :, hd:].reshape((last - first) * M * rows, hd)
        return jnp.dot(weights.astype(BF16), values, preferred_element_type=F32)

    def near():
        scores = scored(0, 2)
        top = jnp.max(scores, axis=1, keepdims=True)
        weights = jnp.exp2(scores - top)
        near_top[...] = jnp.broadcast_to(top, near_top.shape)
        near_norm[...] = jnp.broadcast_to(jnp.sum(weights, axis=1, keepdims=True), near_norm.shape)
        near_out[...] = weighed(weights, 0, 2)

    def store(out):
        for h in range(heads):
            att_ref[:, h * hd : (h + 1) * hd] = out[h * rows : (h + 1) * rows].astype(BF16)

    def far():
        scores = scored(2, reach + 1)
        top = jnp.max(scores, axis=1, keepdims=True)
        weights = jnp.exp2(scores - top)
        norm = jnp.broadcast_to(jnp.sum(weights, axis=1, keepdims=True), near_norm.shape)
        top = jnp.broadcast_to(top, near_top.shape)
        both = jnp.maximum(top, near_top[...])
        keep, keep_near = jnp.exp2(top - both), jnp.exp2(near_top[...] - both)
        norm = norm * keep + near_norm[...] * keep_near
        store((weighed(weights, 2, reach + 1) * keep + near_out[...] * keep_near) / norm)

    ends = jnp.where(g == 0, 0, 2)

    def order(slot):
        mine0, theirs0 = parity * 3, (1 - parity) * 3
        b = theirs0 + 1
        for k, value in enumerate((
            mine0 + ends, blocks - 2 + g, mine0 + 1, theirs0 + 2 - ends, theirs0 + ends, blocks - 1 - g, mine0 + 2 - ends
        )):
            b = jnp.where(slot == k, value, b)
        return b

    def slot_of(b, source_c):
        if b >= blocks - 2:
            return jnp.where(b == blocks - 2 + g, 1, 5)
        par = (g + source_c % 2) % 2
        idx = b % 3
        if idx == 1:
            return jnp.where(par == b // 3, 2, 7)
        same = idx == ends
        return jnp.where(par == b // 3, jnp.where(same, 0, 6), jnp.where(same, 4, 3))

    def t_copy(d, late):
        span = pl.ds(EARLY_PAIRS, blocks // 2 - EARLY_PAIRS) if late else pl.ds(0, EARLY_PAIRS)
        return copy(total.at[span], totals_in.at[d - 1, span], t_send.at[d - 1, late], t_recv.at[d - 1, late], at(place + d))

    def t_start(late):
        def one(d, _):
            t_copy(d, late).start()
            return 0

        lax.fori_loop(1, length - place, one, 0)

    def pass_on(e, ds):
        if e > reach:
            return

        @pl.when(c >= e)
        def _():
            for d in ds:
                k_copy(e, d).wait_recv()

            if e < reach:
                @pl.when(c < C - 1)
                def _():
                    for d in ds:
                        k_copy(e + 1, d).start()

            if ds[-1]:
                r_copy(M - 2 + e, mine).start()

    straight, crossed = (0,), tuple(range(1, M))

    def step(pair, _):
        @pl.when(pair == 0)
        def _():
            pass_on(1, straight)
            relay(0)
            loads[0].wait()
            for d in range(1, M):
                e_copy(d, d).wait_recv()

            @pl.when(c < C - 1)
            def _():
                for d in range(1, M):
                    k_copy(1, d).start()

            for i in range(M - 1):
                r_copy(i, mine).start()
            pass_on(2, straight)
            relay(1)
            pass_on(1, crossed)
            relay(2)
            for d in range(1, M):
                z_copy(d, 0, from_z).wait_recv()
                corner_copy(d, 2 * g + 1 - zb).start()
            loads[1].wait()
            loads[2].wait()

        @pl.when(pair == 1)
        def _():
            for e in range(3, reach + 1):
                pass_on(e, straight)
            relay(3)
            loads[3].wait()
            for i in range(M - 1):
                r_copy(i, other).wait_recv()

            @pl.when(c >= 1)
            def _():
                r_copy(M - 1, other).wait_recv()

            near()
            pass_on(2, crossed)
            arrive(4)
            for d in range(1, M):
                y_copy(d, 1, from_y).wait_recv()
                y_copy(d, 2, from_y).wait_recv()

        @pl.when(pair == 2)
        def _():
            for d in range(1, M):
                z_copy(d, 1, from_z).wait_recv()
                z_copy(d, 2, from_z).wait_recv()
            for e in range(3, reach + 1):
                pass_on(e, crossed)
            for d in range(1, M):
                y_copy(d, 0, from_y).wait_recv()
                corner_copy(d, across).wait_recv()

        @pl.when(pair == 3)
        def _():
            @pl.when(c < C - 1)
            def _():
                pl.semaphore_wait(far_sem, (C - 1 - c) * M)

            t_start(0)
            arrive(5)
            arrive(6)
            for d in range(1, M):
                y_copy(d, 3, from_y).wait_recv()
                z_copy(d, 3, from_z).wait_recv()

        ends_of = [gates(order(2 * pair + k)) for k in range(2)]
        total[pair] = jnp.concatenate(
            [v[:, q : q + 128] for both in ends_of for v in both for q in (0, 128)], axis=0
        )
        return 0

    lax.fori_loop(0, blocks // 2, step, 0)
    t_start(1)

    for e in range(2, reach + 1):
        @pl.when(c >= e)
        def _(e=e):
            r_copy(M - 2 + e, other).wait_recv()

    @pl.when(c < 2)
    def _():
        store(near_out[...] / near_norm[...])

    @pl.when(c >= 2)
    def _():
        far()

    def t_fold(i, entering):
        d = place - i
        t_copy(d, 0).wait_recv()
        t_copy(d, 1).wait_recv()
        new = []
        for b in range(blocks):
            slot = slot_of(b, i // M)
            first = (slot % 2) * 4
            products = totals_in[d - 1, slot // 2, pl.ds(first, 2)]
            new.append(products * entering[b] + totals_in[d - 1, slot // 2, pl.ds(first + 2, 2)])
        return tuple(new)

    entering = lax.fori_loop(0, place, t_fold, (jnp.zeros((2, 128), F32),) * blocks)
    for b in range(blocks):
        for q in range(2):
            first = b * bw + q * 128
            entering_ref[:, first : first + 128] = entering[b][q : q + 1]

    for d in range(1, M):
        e_copy(d).wait_send()
        for i in range(7):
            x_copy(d, i).wait_send()
        for i in range(4):
            y_copy(d, i, own).wait_send()
            z_copy(d, i, own).wait_send()
        corner_copy(d, 2 * g + 1 - zb).wait_send()
    for i in range(M - 1):
        r_copy(i, mine).wait_send()
    for e in range(1, reach + 1):
        @pl.when(c >= e)
        def _(e=e):
            r_copy(M - 2 + e, mine).wait_send()

    for e in range(1, reach + 1):
        @pl.when((c >= e - 1) & (c < C - 1))
        def _(e=e):
            for d in range(M):
                k_copy(e, d).wait_send()

    def t_sent(d, _):
        t_copy(d, 0).wait_send()
        t_copy(d, 1).wait_send()
        return 0

    lax.fori_loop(1, length - place, t_sent, 0)


PIECES = 4


def finish_kernel(att, decay_run, state_run, entering, rec_out, att_out, rec, sem):
    rows = rec.shape[0]
    step = rows // PIECES
    copies = [pltpu.make_async_copy(att, att_out, sem.at[PIECES])]
    copies[0].start()
    for k in range(PIECES):
        here = pl.ds(k * step, step)
        rec[here] = (state_run[here] + decay_run[here] * entering[...]).astype(BF16)
        copies.append(pltpu.make_async_copy(rec.at[here], rec_out.at[here], sem.at[k]))
        copies[-1].start()
    for copy in copies:
        copy.wait()


def on_device(lru_in, gate_weights, decay_param, queries, keys_values):
    G, C, M, R = (lax.axis_size(n) for n in ("groups", "ctx", "mp", "rep"))
    length = C * M
    rows, width = lru_in.shape
    _, blocks, depth, bw = gate_weights.shape
    assert (G, R, C % 2, blocks, bw) == (2, 2, 0, 8, 256)
    reach = min((WINDOW // rows + M - 1) // M, C - 1)
    hd = keys_values.shape[1] // 2
    stacked = rows * (queries.shape[1] // hd)
    dma = pltpu.SemaphoreType.DMA
    anywhere = pl.BlockSpec(memory_space=pltpu.HBM)
    vmem = pl.BlockSpec(memory_space=pltpu.VMEM)
    parts = pl.pallas_call(
        functools.partial(kernel, (C, M)),
        out_shape=(
            pltpu.VMEM(queries.shape, BF16),
            pltpu.VMEM(lru_in.shape, F32),
            pltpu.VMEM(lru_in.shape, F32),
            pltpu.VMEM((1, width), F32),
        ),
        in_specs=[anywhere] * 5,
        out_specs=(vmem,) * 4,
        scratch_shapes=[
            pltpu.VMEM((rows, width), BF16),
            pltpu.VMEM((2, blocks, M, depth, bw), BF16),
            pltpu.VMEM(queries.shape, BF16),
            pltpu.VMEM((reach + 1, M) + keys_values.shape, BF16),
            pltpu.VMEM((stacked, hd), F32),
            pltpu.VMEM((stacked, hd), F32),
            pltpu.VMEM((stacked, hd), F32),
            pltpu.VMEM((1, width), F32),
            pltpu.VMEM((rows, (reach + 1) * M * rows), F32),
            pltpu.VMEM((1, width), F32),
            pltpu.VMEM((blocks // 2, 8, 128), F32),
            pltpu.VMEM((length - 1, blocks // 2, 8, 128), F32),
            dma((5,)),
            dma((M - 1, 7)),
            dma((M - 1, 7)),
            dma((M - 1, 4)),
            dma((M - 1, 4)),
            dma((M - 1, 4)),
            dma((M - 1, 4)),
            dma((M - 1,)),
            dma((M - 1,)),
            dma((M - 1,)),
            dma((M - 1,)),
            dma((reach, M)),
            dma((reach, M)),
            dma((reach + M - 1,)),
            dma((reach + M - 1,)),
            dma((length - 1, 2)),
            dma((length - 1, 2)),
            pltpu.SemaphoreType.REGULAR,
        ],
        compiler_params=pltpu.CompilerParams(
            collective_id=0, has_side_effects=True, vmem_limit_bytes=64 * 2**20 - 917504 - 2440000
        ),
    )(lru_in, gate_weights, decay_param.reshape(1, width), queries, keys_values)
    return pl.pallas_call(
        finish_kernel,
        out_shape=(
            jax.ShapeDtypeStruct(lru_in.shape, BF16),
            jax.ShapeDtypeStruct(queries.shape, BF16),
        ),
        in_specs=[vmem] * 4,
        out_specs=(anywhere, anywhere),
        scratch_shapes=[pltpu.VMEM((rows, width), BF16), dma((PIECES + 1,))],
        compiler_params=pltpu.CompilerParams(vmem_limit_bytes=8 * 2**20),
    )(*parts)


def solution(mesh):
    in_specs = (
        P(("groups", "ctx", "mp"), "rep"),
        P(None, "rep", "mp", None),
        P("rep"),
        P(("groups", "ctx", "mp"), "rep"),
        P(("groups", "ctx", "mp"), None),
    )
    out_specs = (P(("groups", "ctx", "mp"), "rep"), P(("groups", "ctx", "mp"), "rep"))
    return jax.shard_map(
        on_device, mesh=mesh, in_specs=in_specs, out_specs=out_specs, check_vma=False
    )
```

```python
import functools
import math

import jax
import jax.numpy as jnp
from jax import lax
from jax.experimental import pallas as pl
from jax.experimental.pallas import tpu as pltpu
from jax.sharding import PartitionSpec as P

WINDOW = 2048
MESH = pl.DeviceIdType.MESH
F32 = jnp.float32
BF16 = jnp.bfloat16


EARLY_PAIRS = 3


def kernel(
    sizes,
    x_hbm, w_hbm, decay_hbm, q_hbm, kv_hbm,
    att_ref, decay_run, state_run, entering_ref,
    x_ref, wbuf, q_ref, kvbuf, near_top, near_norm, near_out, decay_ref, bias, rate, total, totals_in,
    local_sem, x_send, x_recv, y_send, y_recv, z_send, z_recv, c_send, c_recv,
    e_send, e_recv, k_send, k_recv, r_send, r_recv, t_send, t_recv, far_sem,
):
    C, M = sizes
    length = C * M
    rows, width = x_ref.shape
    blocks, depth, bw = wbuf.shape[1], wbuf.shape[3], wbuf.shape[4]
    reach = kvbuf.shape[0] - 1
    hd = kvbuf.shape[3] // 2
    heads = q_ref.shape[1] // hd
    g, c, m, r = (lax.axis_index(n) for n in ("groups", "ctx", "mp", "rep"))
    place = c * M + m
    zb = c % 2
    twin = c + 1 - 2 * zb
    parity = (g + zb) % 2
    corner = 2 * g + zb
    beside_x = lambda d: (g, c, (m + d) % M, r)
    beside_y = (1 - g, c, m, r)
    beside_z = (g, twin, m, r)
    beside_core = (g, c, m, 1 - r)
    below = lambda e: (g, c + e, m, r)

    def at(position):
        return (g, position // M, position % M, r)

    def signal(sem, device):
        pl.semaphore_signal(sem, inc=1, device_id=device, device_id_type=MESH)

    def copy(src, dst, send, recv, device):
        return pltpu.make_async_remote_copy(
            src_ref=src, dst_ref=dst, send_sem=send, recv_sem=recv, device_id=device, device_id_type=MESH
        )

    loads = [
        pltpu.make_async_copy(kv_hbm, kvbuf.at[0, m], local_sem.at[0]),
        pltpu.make_async_copy(x_hbm, x_ref, local_sem.at[1]),
        pltpu.make_async_copy(w_hbm, wbuf.at[:, :, m], local_sem.at[2]),
        pltpu.make_async_copy(q_hbm, q_ref, local_sem.at[3]),
        pltpu.make_async_copy(decay_hbm, decay_ref, local_sem.at[4]),
    ]

    barrier = pltpu.get_barrier_semaphore()
    for d in range(1, M):
        signal(barrier, beside_x(d))
    signal(barrier, beside_y)
    signal(barrier, beside_core)

    @pl.when(c > 0)
    def _():
        signal(barrier, below(-1))

    def greet_later(i, _):
        signal(barrier, at(i))
        return 0

    lax.fori_loop((c + 1) * M, length, greet_later, 0)

    for load in loads:
        load.start()

    def double(par, first, i):
        i = jnp.where(first == 0, i, 5 - i)
        return i % 2, par * 3 + i // 2

    def single(which):
        return which % 2, blocks - 2 + which // 2

    def tile(par, first, which, i):
        return single(which) if i == 0 else double(par, first, i - 1)

    def own(i):
        return tile(parity, g, corner, i)

    def from_y(i):
        return tile(1 - parity, 1 - g, 2 * (1 - g) + zb, i)

    def from_z(i):
        return tile(1 - parity, g, 2 * g + 1 - zb, i)

    def x_copy(d, i, source=0):
        t, b = own(i)
        return copy(w_hbm.at[t, b], wbuf.at[t, b, (m + M - source) % M], x_send.at[d - 1, i], x_recv.at[d - 1, i], beside_x(d))

    def y_copy(d, i, which):
        t, b = which(i)
        piece = wbuf.at[t, b, (m + M - d) % M]
        return copy(piece, piece, y_send.at[d - 1, i], y_recv.at[d - 1, i], beside_y)

    def z_copy(d, i, which):
        t, b = which(i)
        piece = wbuf.at[t, b, (m + M - d) % M]
        return copy(piece, piece, z_send.at[d - 1, i], z_recv.at[d - 1, i], beside_z)

    across = 3 - corner

    def corner_copy(d, which):
        t, b = single(which)
        piece = wbuf.at[t, b, (m + M - d) % M]
        return copy(piece, piece, c_send.at[d - 1], c_recv.at[d - 1], beside_y)

    def relay(i):
        for d in range(1, M):
            x_copy(d, i, d).wait_recv()
            y_copy(d, i, own).start()
            z_copy(d, i, own).start()

    def arrive(i):
        for d in range(1, M):
            x_copy(d, i, d).wait_recv()

    part = rows // 2
    mine = pl.ds(pl.multiple_of(r * part, part), part)
    other = pl.ds(pl.multiple_of((1 - r) * part, part), part)

    def e_copy(d, source=0):
        return copy(kv_hbm.at[mine], kvbuf.at[0, (m + M - source) % M, mine], e_send.at[d - 1], e_recv.at[d - 1], beside_x(d))

    def k_copy(e, d):
        piece = (m + d) % M
        src = kv_hbm.at[mine] if (e, d) == (1, 0) else kvbuf.at[e - 1, piece, mine]
        return copy(src, kvbuf.at[e, piece, mine], k_send.at[e - 1, d], k_recv.at[e - 1, d], below(1))

    def r_copy(i, rows_of):
        piece = kvbuf.at[0, (m + i + 1) % M, rows_of] if i < M - 1 else kvbuf.at[i - M + 2, :, rows_of]
        return copy(piece, piece, r_send.at[i], r_recv.at[i], beside_core)

    pl.semaphore_wait(barrier, M + 1 + c * M + (c < C - 1).astype(jnp.int32))

    for d in range(1, M):
        x_copy(d, 0).start()
    for d in range(1, M):
        e_copy(d).start()
    for i in range(1, 7):
        for d in range(1, M):
            x_copy(d, i).start()

    @pl.when(c < C - 1)
    def _():
        k_copy(1, 0).start()

    def greet(i, _):
        signal(far_sem, at(i))
        return 0

    lax.fori_loop(0, c * M, greet, 0)

    for e in range(1, reach + 1):
        @pl.when(c < e)
        def _(e=e):
            kvbuf[e] = jnp.zeros(kvbuf.shape[1:], BF16)


    loads[4].wait()
    e = jnp.exp(-decay_ref[...])
    s = e / (2.0 + e)
    s2 = s * s
    rate[...] = -16.0 * s * (1.0 + s2 * (1.0 / 3.0 + s2 * (1.0 / 5.0)))

    row = lax.broadcasted_iota(jnp.int32, (rows, rows), 0)
    col = lax.broadcasted_iota(jnp.int32, (rows, rows), 1)
    for e in range(reach + 1):
        for n in range(M):
            back = row - col + (e * M + m - n) * rows
            allowed = (back >= 0) & (back < WINDOW) & (c >= e)
            first = (e * M + n) * rows
            bias[:, first : first + rows] = jnp.where(allowed, 0.0, -1e30).astype(F32)

    groups8 = rows // 8
    sub = lax.broadcasted_iota(jnp.int32, (groups8, 8, bw), 1)

    def gates(b):
        lanes = pl.ds(pl.multiple_of(b * bw, bw), bw)
        xb = x_ref[:, lanes]
        g0 = jnp.dot(xb, wbuf[0, b].reshape(bw, bw), preferred_element_type=F32)
        g1 = jnp.dot(xb, wbuf[1, b].reshape(bw, bw), preferred_element_type=F32)
        y = rate[:, lanes] * jax.nn.sigmoid(g0)
        poly = 1.0 + y * (1 / 2 + y * (1 / 6 + y * (1 / 24 + y * (1 / 120 + y * (1 / 720)))))
        u = y * poly
        a = (1.0 + u).reshape(groups8, 8, bw)
        v = jnp.sqrt(-u * (2.0 + u)) * jax.nn.sigmoid(g1) * xb.astype(F32)
        v = v.reshape(groups8, 8, bw)
        for shift in (1, 2, 4):
            keep = sub >= shift
            before_v = jnp.where(keep, pltpu.roll(v, shift, 1), 0.0)
            before_a = jnp.where(keep, pltpu.roll(a, shift, 1), 1.0)
            v = a * before_v + v
            a = a * before_a
        ta, tv = jnp.ones((1, bw), F32), jnp.zeros((1, bw), F32)
        for k in range(groups8):
            here = slice(k * 8, k * 8 + 8)
            vk = a[k] * tv + v[k]
            ak = a[k] * ta
            decay_run[here, lanes] = ak
            state_run[here, lanes] = vk
            ta, tv = ak[7:8], vk[7:8]
        return ta, tv

    scale = math.log2(math.e) / math.sqrt(hd)

    def scored(first, last):
        count = (last - first) * M * rows
        q = jnp.concatenate([q_ref[:, h * hd : (h + 1) * hd] for h in range(heads)], axis=0)
        keys = kvbuf[first:last, :, :, :hd].reshape(count, hd)
        scores = lax.dot_general(q, keys, (((1,), (1,)), ((), ())), preferred_element_type=F32)
        scores = scores.reshape(heads, rows, count) * scale + bias[:, first * M * rows : last * M * rows]
        return scores.reshape(heads * rows, count)

    def weighed(weights, first, last):
        values = kvbuf[first:last, :, :, hd:].reshape((last - first) * M * rows, hd)
        return jnp.dot(weights.astype(BF16), values, preferred_element_type=F32)

    def near():
        scores = scored(0, 2)
        top = jnp.max(scores, axis=1, keepdims=True)
        weights = jnp.exp2(scores - top)
        near_top[...] = jnp.broadcast_to(top, near_top.shape)
        near_norm[...] = jnp.broadcast_to(jnp.sum(weights, axis=1, keepdims=True), near_norm.shape)
        near_out[...] = weighed(weights, 0, 2)

    def store(out):
        for h in range(heads):
            att_ref[:, h * hd : (h + 1) * hd] = out[h * rows : (h + 1) * rows].astype(BF16)

    def further(e, last):
        scores = scored(e, e + 1)
        top = jnp.max(scores, axis=1, keepdims=True)
        weights = jnp.exp2(scores - top)
        norm = jnp.broadcast_to(jnp.sum(weights, axis=1, keepdims=True), near_norm.shape)
        top = jnp.broadcast_to(top, near_top.shape)
        both = jnp.maximum(top, near_top[...])
        keep, keep_near = jnp.exp2(top - both), jnp.exp2(near_top[...] - both)
        norm = norm * keep + near_norm[...] * keep_near
        out = weighed(weights, e, e + 1) * keep + near_out[...] * keep_near
        if last:
            store(out / norm)
        else:
            near_top[...] = both
            near_norm[...] = norm
            near_out[...] = out

    ends = jnp.where(g == 0, 0, 2)

    def order(slot):
        mine0, theirs0 = parity * 3, (1 - parity) * 3
        b = theirs0 + 1
        for k, value in enumerate((
            mine0 + ends, blocks - 2 + g, mine0 + 1, theirs0 + 2 - ends, theirs0 + ends, blocks - 1 - g, mine0 + 2 - ends
        )):
            b = jnp.where(slot == k, value, b)
        return b

    def slot_of(b, source_c):
        if b >= blocks - 2:
            return jnp.where(b == blocks - 2 + g, 1, 5)
        par = (g + source_c % 2) % 2
        idx = b % 3
        if idx == 1:
            return jnp.where(par == b // 3, 2, 7)
        same = idx == ends
        return jnp.where(par == b // 3, jnp.where(same, 0, 6), jnp.where(same, 4, 3))

    def t_copy(d, late):
        span = pl.ds(EARLY_PAIRS, blocks // 2 - EARLY_PAIRS) if late else pl.ds(0, EARLY_PAIRS)
        return copy(total.at[span], totals_in.at[d - 1, span], t_send.at[d - 1, late], t_recv.at[d - 1, late], at(place + d))

    def t_start(late):
        def one(d, _):
            t_copy(d, late).start()
            return 0

        lax.fori_loop(1, length - place, one, 0)

    def pass_on(e, ds):
        if e > reach:
            return

        @pl.when(c >= e)
        def _():
            for d in ds:
                k_copy(e, d).wait_recv()

            if e < reach:
                @pl.when(c < C - 1)
                def _():
                    for d in ds:
                        k_copy(e + 1, d).start()

            if ds[-1]:
                r_copy(M - 2 + e, mine).start()

    straight, crossed = (0,), tuple(range(1, M))

    def step(pair, _):
        @pl.when(pair == 0)
        def _():
            pass_on(1, straight)
            relay(0)
            loads[0].wait()
            for d in range(1, M):
                e_copy(d, d).wait_recv()

            @pl.when(c < C - 1)
            def _():
                for d in range(1, M):
                    k_copy(1, d).start()

            for i in range(M - 1):
                r_copy(i, mine).start()
            pass_on(2, straight)
            relay(1)
            pass_on(1, crossed)
            relay(2)
            for d in range(1, M):
                z_copy(d, 0, from_z).wait_recv()
                corner_copy(d, 2 * g + 1 - zb).start()
            loads[1].wait()
            loads[2].wait()

        @pl.when(pair == 1)
        def _():
            for e in range(3, reach + 1):
                pass_on(e, straight)
            relay(3)
            pass_on(2, crossed)
            loads[3].wait()
            for i in range(M - 1):
                r_copy(i, other).wait_recv()

            @pl.when(c >= 1)
            def _():
                r_copy(M - 1, other).wait_recv()

            near()
            arrive(4)
            for d in range(1, M):
                y_copy(d, 1, from_y).wait_recv()
                y_copy(d, 2, from_y).wait_recv()

        @pl.when(pair == 2)
        def _():
            for d in range(1, M):
                z_copy(d, 1, from_z).wait_recv()
                z_copy(d, 2, from_z).wait_recv()
            for e in range(3, reach + 1):
                pass_on(e, crossed)
            for d in range(1, M):
                y_copy(d, 0, from_y).wait_recv()
                corner_copy(d, across).wait_recv()

        @pl.when(pair == 3)
        def _():
            @pl.when(c < C - 1)
            def _():
                pl.semaphore_wait(far_sem, (C - 1 - c) * M)

            t_start(0)
            arrive(5)
            arrive(6)
            for d in range(1, M):
                y_copy(d, 3, from_y).wait_recv()
                z_copy(d, 3, from_z).wait_recv()

        ends_of = [gates(order(2 * pair + k)) for k in range(2)]
        total[pair] = jnp.concatenate(
            [v[:, q : q + 128] for both in ends_of for v in both for q in (0, 128)], axis=0
        )
        return 0

    lax.fori_loop(0, blocks // 2, step, 0)
    t_start(1)

    for e in range(2, reach + 1):
        @pl.when(c >= e)
        def _(e=e):
            r_copy(M - 2 + e, other).wait_recv()
            further(e, e == reach)

    @pl.when(c < reach)
    def _():
        store(near_out[...] / near_norm[...])

    def t_fold(i, entering):
        d = place - i
        t_copy(d, 0).wait_recv()
        t_copy(d, 1).wait_recv()
        new = []
        for b in range(blocks):
            slot = slot_of(b, i // M)
            first = (slot % 2) * 4
            products = totals_in[d - 1, slot // 2, pl.ds(first, 2)]
            new.append(products * entering[b] + totals_in[d - 1, slot // 2, pl.ds(first + 2, 2)])
        return tuple(new)

    entering = lax.fori_loop(0, place, t_fold, (jnp.zeros((2, 128), F32),) * blocks)
    for b in range(blocks):
        for q in range(2):
            first = b * bw + q * 128
            entering_ref[:, first : first + 128] = entering[b][q : q + 1]

    for d in range(1, M):
        e_copy(d).wait_send()
        for i in range(7):
            x_copy(d, i).wait_send()
        for i in range(4):
            y_copy(d, i, own).wait_send()
            z_copy(d, i, own).wait_send()
        corner_copy(d, 2 * g + 1 - zb).wait_send()
    for i in range(M - 1):
        r_copy(i, mine).wait_send()
    for e in range(1, reach + 1):
        @pl.when(c >= e)
        def _(e=e):
            r_copy(M - 2 + e, mine).wait_send()

    for e in range(1, reach + 1):
        @pl.when((c >= e - 1) & (c < C - 1))
        def _(e=e):
            for d in range(M):
                k_copy(e, d).wait_send()

    def t_sent(d, _):
        t_copy(d, 0).wait_send()
        t_copy(d, 1).wait_send()
        return 0

    lax.fori_loop(1, length - place, t_sent, 0)


PIECES = 4


def finish_kernel(att, decay_run, state_run, entering, rec_out, att_out, rec, sem):
    rows = rec.shape[0]
    step = rows // PIECES
    copies = [pltpu.make_async_copy(att, att_out, sem.at[PIECES])]
    copies[0].start()
    for k in range(PIECES):
        here = pl.ds(k * step, step)
        rec[here] = (state_run[here] + decay_run[here] * entering[...]).astype(BF16)
        copies.append(pltpu.make_async_copy(rec.at[here], rec_out.at[here], sem.at[k]))
        copies[-1].start()
    for copy in copies:
        copy.wait()


def on_device(lru_in, gate_weights, decay_param, queries, keys_values):
    G, C, M, R = (lax.axis_size(n) for n in ("groups", "ctx", "mp", "rep"))
    length = C * M
    rows, width = lru_in.shape
    _, blocks, depth, bw = gate_weights.shape
    assert (G, R, C % 2, blocks, bw) == (2, 2, 0, 8, 256)
    reach = min((WINDOW // rows + M - 1) // M, C - 1)
    hd = keys_values.shape[1] // 2
    stacked = rows * (queries.shape[1] // hd)
    dma = pltpu.SemaphoreType.DMA
    anywhere = pl.BlockSpec(memory_space=pltpu.HBM)
    vmem = pl.BlockSpec(memory_space=pltpu.VMEM)
    parts = pl.pallas_call(
        functools.partial(kernel, (C, M)),
        out_shape=(
            pltpu.VMEM(queries.shape, BF16),
            pltpu.VMEM(lru_in.shape, F32),
            pltpu.VMEM(lru_in.shape, F32),
            pltpu.VMEM((1, width), F32),
        ),
        in_specs=[anywhere] * 5,
        out_specs=(vmem,) * 4,
        scratch_shapes=[
            pltpu.VMEM((rows, width), BF16),
            pltpu.VMEM((2, blocks, M, depth, bw), BF16),
            pltpu.VMEM(queries.shape, BF16),
            pltpu.VMEM((reach + 1, M) + keys_values.shape, BF16),
            pltpu.VMEM((stacked, hd), F32),
            pltpu.VMEM((stacked, hd), F32),
            pltpu.VMEM((stacked, hd), F32),
            pltpu.VMEM((1, width), F32),
            pltpu.VMEM((rows, (reach + 1) * M * rows), F32),
            pltpu.VMEM((1, width), F32),
            pltpu.VMEM((blocks // 2, 8, 128), F32),
            pltpu.VMEM((length - 1, blocks // 2, 8, 128), F32),
            dma((5,)),
            dma((M - 1, 7)),
            dma((M - 1, 7)),
            dma((M - 1, 4)),
            dma((M - 1, 4)),
            dma((M - 1, 4)),
            dma((M - 1, 4)),
            dma((M - 1,)),
            dma((M - 1,)),
            dma((M - 1,)),
            dma((M - 1,)),
            dma((reach, M)),
            dma((reach, M)),
            dma((reach + M - 1,)),
            dma((reach + M - 1,)),
            dma((length - 1, 2)),
            dma((length - 1, 2)),
            pltpu.SemaphoreType.REGULAR,
        ],
        compiler_params=pltpu.CompilerParams(
            collective_id=0, has_side_effects=True, vmem_limit_bytes=64 * 2**20 - 917504 - 2440000
        ),
    )(lru_in, gate_weights, decay_param.reshape(1, width), queries, keys_values)
    return pl.pallas_call(
        finish_kernel,
        out_shape=(
            jax.ShapeDtypeStruct(lru_in.shape, BF16),
            jax.ShapeDtypeStruct(queries.shape, BF16),
        ),
        in_specs=[vmem] * 4,
        out_specs=(anywhere, anywhere),
        scratch_shapes=[pltpu.VMEM((rows, width), BF16), dma((PIECES + 1,))],
        compiler_params=pltpu.CompilerParams(vmem_limit_bytes=8 * 2**20),
    )(*parts)


def solution(mesh):
    in_specs = (
        P(("groups", "ctx", "mp"), "rep"),
        P(None, "rep", "mp", None),
        P("rep"),
        P(("groups", "ctx", "mp"), "rep"),
        P(("groups", "ctx", "mp"), None),
    )
    out_specs = (P(("groups", "ctx", "mp"), "rep"), P(("groups", "ctx", "mp"), "rep"))
    return jax.shard_map(
        on_device, mesh=mesh, in_specs=in_specs, out_specs=out_specs, check_vma=False
    )
```

```python
import functools
import math

import jax
import jax.numpy as jnp
from jax import lax
from jax.experimental import pallas as pl
from jax.experimental.pallas import tpu as pltpu
from jax.sharding import PartitionSpec as P

WINDOW = 2048
MESH = pl.DeviceIdType.MESH
F32 = jnp.float32
BF16 = jnp.bfloat16


EARLY_PAIRS = 3


def kernel(
    sizes,
    x_hbm, w_hbm, decay_hbm, q_hbm, kv_hbm,
    att_ref, decay_run, state_run, entering_ref,
    x_ref, wbuf, q_ref, kvbuf, near_top, near_norm, near_out, decay_ref, bias, rate, total, totals_in,
    local_sem, x_send, x_recv, y_send, y_recv, z_send, z_recv, c_send, c_recv,
    e_send, e_recv, k_send, k_recv, r_send, r_recv, t_send, t_recv, far_sem,
):
    C, M = sizes
    length = C * M
    rows, width = x_ref.shape
    blocks, depth, bw = wbuf.shape[1], wbuf.shape[3], wbuf.shape[4]
    reach = kvbuf.shape[0] - 1
    hd = kvbuf.shape[3] // 2
    heads = q_ref.shape[1] // hd
    g, c, m, r = (lax.axis_index(n) for n in ("groups", "ctx", "mp", "rep"))
    place = c * M + m
    zb = c % 2
    twin = c + 1 - 2 * zb
    parity = (g + zb) % 2
    corner = 2 * g + zb
    beside_x = lambda d: (g, c, (m + d) % M, r)
    beside_y = (1 - g, c, m, r)
    beside_z = (g, twin, m, r)
    beside_core = (g, c, m, 1 - r)
    below = lambda e: (g, c + e, m, r)

    def at(position):
        return (g, position // M, position % M, r)

    def signal(sem, device):
        pl.semaphore_signal(sem, inc=1, device_id=device, device_id_type=MESH)

    def copy(src, dst, send, recv, device):
        return pltpu.make_async_remote_copy(
            src_ref=src, dst_ref=dst, send_sem=send, recv_sem=recv, device_id=device, device_id_type=MESH
        )

    loads = [
        pltpu.make_async_copy(kv_hbm, kvbuf.at[0, m], local_sem.at[0]),
        pltpu.make_async_copy(x_hbm, x_ref, local_sem.at[1]),
        pltpu.make_async_copy(w_hbm, wbuf.at[:, :, m], local_sem.at[2]),
        pltpu.make_async_copy(q_hbm, q_ref, local_sem.at[3]),
        pltpu.make_async_copy(decay_hbm, decay_ref, local_sem.at[4]),
    ]

    barrier = pltpu.get_barrier_semaphore()
    for d in range(1, M):
        signal(barrier, beside_x(d))
    signal(barrier, beside_y)
    signal(barrier, beside_core)

    @pl.when(c > 0)
    def _():
        signal(barrier, below(-1))

    def greet_later(i, _):
        signal(barrier, at(i))
        return 0

    lax.fori_loop((c + 1) * M, length, greet_later, 0)

    for load in loads:
        load.start()

    def double(par, first, i):
        i = jnp.where(first == 0, i, 5 - i)
        return i % 2, par * 3 + i // 2

    def single(which):
        return which % 2, blocks - 2 + which // 2

    def tile(par, first, which, i):
        return single(which) if i == 0 else double(par, first, i - 1)

    def own(i):
        return tile(parity, g, corner, i)

    def from_y(i):
        return tile(1 - parity, 1 - g, 2 * (1 - g) + zb, i)

    def from_z(i):
        return tile(1 - parity, g, 2 * g + 1 - zb, i)

    def x_copy(d, i, source=0):
        t, b = own(i)
        return copy(w_hbm.at[t, b], wbuf.at[t, b, (m + M - source) % M], x_send.at[d - 1, i], x_recv.at[d - 1, i], beside_x(d))

    def y_copy(d, i, which):
        t, b = which(i)
        piece = wbuf.at[t, b, (m + M - d) % M]
        return copy(piece, piece, y_send.at[d - 1, i], y_recv.at[d - 1, i], beside_y)

    def z_copy(d, i, which):
        t, b = which(i)
        piece = wbuf.at[t, b, (m + M - d) % M]
        return copy(piece, piece, z_send.at[d - 1, i], z_recv.at[d - 1, i], beside_z)

    across = 3 - corner

    def corner_copy(d, which):
        t, b = single(which)
        piece = wbuf.at[t, b, (m + M - d) % M]
        return copy(piece, piece, c_send.at[d - 1], c_recv.at[d - 1], beside_y)

    def relay(i):
        for d in range(1, M):
            x_copy(d, i, d).wait_recv()
            y_copy(d, i, own).start()
            z_copy(d, i, own).start()

    def arrive(i):
        for d in range(1, M):
            x_copy(d, i, d).wait_recv()

    part = rows // 2
    mine = pl.ds(pl.multiple_of(r * part, part), part)
    other = pl.ds(pl.multiple_of((1 - r) * part, part), part)

    def e_copy(d, source=0):
        return copy(kv_hbm.at[mine], kvbuf.at[0, (m + M - source) % M, mine], e_send.at[d - 1], e_recv.at[d - 1], beside_x(d))

    def k_copy(e, d):
        piece = (m + d) % M
        src = kv_hbm.at[mine] if (e, d) == (1, 0) else kvbuf.at[e - 1, piece, mine]
        return copy(src, kvbuf.at[e, piece, mine], k_send.at[e - 1, d], k_recv.at[e - 1, d], below(1))

    def r_copy(i, rows_of):
        piece = kvbuf.at[0, (m + i + 1) % M, rows_of] if i < M - 1 else kvbuf.at[i - M + 2, :, rows_of]
        return copy(piece, piece, r_send.at[i], r_recv.at[i], beside_core)

    pl.semaphore_wait(barrier, M + 1 + c * M + (c < C - 1).astype(jnp.int32))

    for d in range(1, M):
        x_copy(d, 0).start()
    for d in range(1, M):
        e_copy(d).start()
    for i in range(1, 7):
        for d in range(1, M):
            x_copy(d, i).start()

    @pl.when(c < C - 1)
    def _():
        k_copy(1, 0).start()

    def greet(i, _):
        signal(far_sem, at(i))
        return 0

    lax.fori_loop(0, c * M, greet, 0)

    for e in range(1, reach + 1):
        @pl.when(c < e)
        def _(e=e):
            kvbuf[e] = jnp.zeros(kvbuf.shape[1:], BF16)


    loads[4].wait()
    e = jnp.exp(-decay_ref[...])
    s = e / (2.0 + e)
    s2 = s * s
    rate[...] = -16.0 * s * (1.0 + s2 * (1.0 / 3.0 + s2 * (1.0 / 5.0)))

    row = lax.broadcasted_iota(jnp.int32, (rows, rows), 0)
    col = lax.broadcasted_iota(jnp.int32, (rows, rows), 1)
    for e in range(reach + 1):
        for n in range(M):
            back = row - col + (e * M + m - n) * rows
            allowed = (back >= 0) & (back < WINDOW) & (c >= e)
            first = (e * M + n) * rows
            bias[:, first : first + rows] = jnp.where(allowed, 0.0, -1e30).astype(F32)

    groups8 = rows // 8
    sub = lax.broadcasted_iota(jnp.int32, (groups8, 8, bw), 1)

    def gates(b):
        lanes = pl.ds(pl.multiple_of(b * bw, bw), bw)
        xb = x_ref[:, lanes]
        g0 = jnp.dot(xb, wbuf[0, b].reshape(bw, bw), preferred_element_type=F32)
        g1 = jnp.dot(xb, wbuf[1, b].reshape(bw, bw), preferred_element_type=F32)
        y = rate[:, lanes] * jax.nn.sigmoid(g0)
        poly = 1.0 + y * (1 / 2 + y * (1 / 6 + y * (1 / 24 + y * (1 / 120 + y * (1 / 720)))))
        u = y * poly
        a = (1.0 + u).reshape(groups8, 8, bw)
        v = jnp.sqrt(-u * (2.0 + u)) * jax.nn.sigmoid(g1) * xb.astype(F32)
        v = v.reshape(groups8, 8, bw)
        for shift in (1, 2, 4):
            keep = sub >= shift
            before_v = jnp.where(keep, pltpu.roll(v, shift, 1), 0.0)
            before_a = jnp.where(keep, pltpu.roll(a, shift, 1), 1.0)
            v = a * before_v + v
            a = a * before_a
        ta, tv = jnp.ones((1, bw), F32), jnp.zeros((1, bw), F32)
        for k in range(groups8):
            here = slice(k * 8, k * 8 + 8)
            vk = a[k] * tv + v[k]
            ak = a[k] * ta
            decay_run[here, lanes] = ak
            state_run[here, lanes] = vk
            ta, tv = ak[7:8], vk[7:8]
        return ta, tv

    scale = math.log2(math.e) / math.sqrt(hd)

    def scored(first, last):
        count = (last - first) * M * rows
        q = jnp.concatenate([q_ref[:, h * hd : (h + 1) * hd] for h in range(heads)], axis=0)
        keys = kvbuf[first:last, :, :, :hd].reshape(count, hd)
        scores = lax.dot_general(q, keys, (((1,), (1,)), ((), ())), preferred_element_type=F32)
        scores = scores.reshape(heads, rows, count) * scale + bias[:, first * M * rows : last * M * rows]
        return scores.reshape(heads * rows, count)

    def weighed(weights, first, last):
        values = kvbuf[first:last, :, :, hd:].reshape((last - first) * M * rows, hd)
        return jnp.dot(weights.astype(BF16), values, preferred_element_type=F32)

    def near():
        scores = scored(0, 2)
        top = jnp.max(scores, axis=1, keepdims=True)
        weights = jnp.exp2(scores - top)
        near_top[...] = jnp.broadcast_to(top, near_top.shape)
        near_norm[...] = jnp.broadcast_to(jnp.sum(weights, axis=1, keepdims=True), near_norm.shape)
        near_out[...] = weighed(weights, 0, 2)

    def store(out):
        for h in range(heads):
            att_ref[:, h * hd : (h + 1) * hd] = out[h * rows : (h + 1) * rows].astype(BF16)

    def further(e, last):
        scores = scored(e, e + 1)
        top = jnp.max(scores, axis=1, keepdims=True)
        weights = jnp.exp2(scores - top)
        norm = jnp.broadcast_to(jnp.sum(weights, axis=1, keepdims=True), near_norm.shape)
        top = jnp.broadcast_to(top, near_top.shape)
        both = jnp.maximum(top, near_top[...])
        keep, keep_near = jnp.exp2(top - both), jnp.exp2(near_top[...] - both)
        norm = norm * keep + near_norm[...] * keep_near
        out = weighed(weights, e, e + 1) * keep + near_out[...] * keep_near
        if last:
            store(out / norm)
        else:
            near_top[...] = both
            near_norm[...] = norm
            near_out[...] = out

    ends = jnp.where(g == 0, 0, 2)

    def order(slot):
        mine0, theirs0 = parity * 3, (1 - parity) * 3
        b = theirs0 + 1
        for k, value in enumerate((
            mine0 + ends, blocks - 2 + g, mine0 + 1, theirs0 + 2 - ends, theirs0 + ends, blocks - 1 - g, mine0 + 2 - ends
        )):
            b = jnp.where(slot == k, value, b)
        return b

    def slot_of(b, source_c):
        if b >= blocks - 2:
            return jnp.where(b == blocks - 2 + g, 1, 5)
        par = (g + source_c % 2) % 2
        idx = b % 3
        if idx == 1:
            return jnp.where(par == b // 3, 2, 7)
        same = idx == ends
        return jnp.where(par == b // 3, jnp.where(same, 0, 6), jnp.where(same, 4, 3))

    def t_copy(d, late):
        span = pl.ds(EARLY_PAIRS, blocks // 2 - EARLY_PAIRS) if late else pl.ds(0, EARLY_PAIRS)
        return copy(total.at[span], totals_in.at[d - 1, span], t_send.at[d - 1, late], t_recv.at[d - 1, late], at(place + d))

    def t_start(late):
        def one(d, _):
            t_copy(d, late).start()
            return 0

        for d in range(1, min(length, 8)):
            @pl.when(place + d < length)
            def _(d=d):
                t_copy(d, late).start()

        lax.fori_loop(8, length - place, one, 0)

    def pass_on(e, ds):
        if e > reach:
            return

        @pl.when(c >= e)
        def _():
            for d in ds:
                k_copy(e, d).wait_recv()

            if e < reach:
                @pl.when(c < C - 1)
                def _():
                    for d in ds:
                        k_copy(e + 1, d).start()

            if ds[-1]:
                r_copy(M - 2 + e, mine).start()

    straight, crossed = (0,), tuple(range(1, M))

    def step(pair, _):
        @pl.when(pair == 0)
        def _():
            pass_on(1, straight)
            relay(0)
            loads[0].wait()
            for d in range(1, M):
                e_copy(d, d).wait_recv()

            @pl.when(c < C - 1)
            def _():
                for d in range(1, M):
                    k_copy(1, d).start()

            for i in range(M - 1):
                r_copy(i, mine).start()
            pass_on(2, straight)
            relay(1)
            pass_on(1, crossed)
            relay(2)
            for d in range(1, M):
                z_copy(d, 0, from_z).wait_recv()
                corner_copy(d, 2 * g + 1 - zb).start()
            loads[1].wait()
            loads[2].wait()

        @pl.when(pair == 1)
        def _():
            for e in range(3, reach + 1):
                pass_on(e, straight)
            relay(3)
            pass_on(2, crossed)
            loads[3].wait()
            for i in range(M - 1):
                r_copy(i, other).wait_recv()

            @pl.when(c >= 1)
            def _():
                r_copy(M - 1, other).wait_recv()

            near()
            arrive(4)
            for d in range(1, M):
                y_copy(d, 1, from_y).wait_recv()
                y_copy(d, 2, from_y).wait_recv()

        @pl.when(pair == 2)
        def _():
            for d in range(1, M):
                z_copy(d, 1, from_z).wait_recv()
                z_copy(d, 2, from_z).wait_recv()
            for e in range(3, reach + 1):
                pass_on(e, crossed)
            for d in range(1, M):
                y_copy(d, 0, from_y).wait_recv()
                corner_copy(d, across).wait_recv()

        @pl.when(pair == 3)
        def _():
            @pl.when(c < C - 1)
            def _():
                pl.semaphore_wait(far_sem, (C - 1 - c) * M)

            t_start(0)
            arrive(5)
            arrive(6)
            for d in range(1, M):
                y_copy(d, 3, from_y).wait_recv()
                z_copy(d, 3, from_z).wait_recv()

        ends_of = [gates(order(2 * pair + k)) for k in range(2)]
        total[pair] = jnp.concatenate(
            [v[:, q : q + 128] for both in ends_of for v in both for q in (0, 128)], axis=0
        )
        return 0

    lax.fori_loop(0, blocks // 2, step, 0)
    t_start(1)

    for e in range(2, reach + 1):
        @pl.when(c >= e)
        def _(e=e):
            r_copy(M - 2 + e, other).wait_recv()
            further(e, e == reach)

    @pl.when(c < reach)
    def _():
        store(near_out[...] / near_norm[...])

    def t_fold(i, entering):
        d = place - i
        t_copy(d, 0).wait_recv()
        t_copy(d, 1).wait_recv()
        new = []
        for b in range(blocks):
            slot = slot_of(b, i // M)
            first = (slot % 2) * 4
            products = totals_in[d - 1, slot // 2, pl.ds(first, 2)]
            new.append(products * entering[b] + totals_in[d - 1, slot // 2, pl.ds(first + 2, 2)])
        return tuple(new)

    entering = lax.fori_loop(0, place, t_fold, (jnp.zeros((2, 128), F32),) * blocks)
    for b in range(blocks):
        for q in range(2):
            first = b * bw + q * 128
            entering_ref[:, first : first + 128] = entering[b][q : q + 1]

    for d in range(1, M):
        e_copy(d).wait_send()
        for i in range(7):
            x_copy(d, i).wait_send()
        for i in range(4):
            y_copy(d, i, own).wait_send()
            z_copy(d, i, own).wait_send()
        corner_copy(d, 2 * g + 1 - zb).wait_send()
    for i in range(M - 1):
        r_copy(i, mine).wait_send()
    for e in range(1, reach + 1):
        @pl.when(c >= e)
        def _(e=e):
            r_copy(M - 2 + e, mine).wait_send()

    for e in range(1, reach + 1):
        @pl.when((c >= e - 1) & (c < C - 1))
        def _(e=e):
            for d in range(M):
                k_copy(e, d).wait_send()

    def t_sent(d, _):
        t_copy(d, 0).wait_send()
        t_copy(d, 1).wait_send()
        return 0

    lax.fori_loop(1, length - place, t_sent, 0)


PIECES = 4


def finish_kernel(att, decay_run, state_run, entering, rec_out, att_out, rec, sem):
    rows = rec.shape[0]
    step = rows // PIECES
    copies = [pltpu.make_async_copy(att, att_out, sem.at[PIECES])]
    copies[0].start()
    for k in range(PIECES):
        here = pl.ds(k * step, step)
        rec[here] = (state_run[here] + decay_run[here] * entering[...]).astype(BF16)
        copies.append(pltpu.make_async_copy(rec.at[here], rec_out.at[here], sem.at[k]))
        copies[-1].start()
    for copy in copies:
        copy.wait()


def on_device(lru_in, gate_weights, decay_param, queries, keys_values):
    G, C, M, R = (lax.axis_size(n) for n in ("groups", "ctx", "mp", "rep"))
    length = C * M
    rows, width = lru_in.shape
    _, blocks, depth, bw = gate_weights.shape
    assert (G, R, C % 2, blocks, bw) == (2, 2, 0, 8, 256)
    reach = min((WINDOW // rows + M - 1) // M, C - 1)
    hd = keys_values.shape[1] // 2
    stacked = rows * (queries.shape[1] // hd)
    dma = pltpu.SemaphoreType.DMA
    anywhere = pl.BlockSpec(memory_space=pltpu.HBM)
    vmem = pl.BlockSpec(memory_space=pltpu.VMEM)
    parts = pl.pallas_call(
        functools.partial(kernel, (C, M)),
        out_shape=(
            pltpu.VMEM(queries.shape, BF16),
            pltpu.VMEM(lru_in.shape, F32),
            pltpu.VMEM(lru_in.shape, F32),
            pltpu.VMEM((1, width), F32),
        ),
        in_specs=[anywhere] * 5,
        out_specs=(vmem,) * 4,
        scratch_shapes=[
            pltpu.VMEM((rows, width), BF16),
            pltpu.VMEM((2, blocks, M, depth, bw), BF16),
            pltpu.VMEM(queries.shape, BF16),
            pltpu.VMEM((reach + 1, M) + keys_values.shape, BF16),
            pltpu.VMEM((stacked, hd), F32),
            pltpu.VMEM((stacked, hd), F32),
            pltpu.VMEM((stacked, hd), F32),
            pltpu.VMEM((1, width), F32),
            pltpu.VMEM((rows, (reach + 1) * M * rows), F32),
            pltpu.VMEM((1, width), F32),
            pltpu.VMEM((blocks // 2, 8, 128), F32),
            pltpu.VMEM((length - 1, blocks // 2, 8, 128), F32),
            dma((5,)),
            dma((M - 1, 7)),
            dma((M - 1, 7)),
            dma((M - 1, 4)),
            dma((M - 1, 4)),
            dma((M - 1, 4)),
            dma((M - 1, 4)),
            dma((M - 1,)),
            dma((M - 1,)),
            dma((M - 1,)),
            dma((M - 1,)),
            dma((reach, M)),
            dma((reach, M)),
            dma((reach + M - 1,)),
            dma((reach + M - 1,)),
            dma((length - 1, 2)),
            dma((length - 1, 2)),
            pltpu.SemaphoreType.REGULAR,
        ],
        compiler_params=pltpu.CompilerParams(
            collective_id=0, has_side_effects=True, vmem_limit_bytes=64 * 2**20 - 917504 - 2440000
        ),
    )(lru_in, gate_weights, decay_param.reshape(1, width), queries, keys_values)
    return pl.pallas_call(
        finish_kernel,
        out_shape=(
            jax.ShapeDtypeStruct(lru_in.shape, BF16),
            jax.ShapeDtypeStruct(queries.shape, BF16),
        ),
        in_specs=[vmem] * 4,
        out_specs=(anywhere, anywhere),
        scratch_shapes=[pltpu.VMEM((rows, width), BF16), dma((PIECES + 1,))],
        compiler_params=pltpu.CompilerParams(vmem_limit_bytes=8 * 2**20),
    )(*parts)


def solution(mesh):
    in_specs = (
        P(("groups", "ctx", "mp"), "rep"),
        P(None, "rep", "mp", None),
        P("rep"),
        P(("groups", "ctx", "mp"), "rep"),
        P(("groups", "ctx", "mp"), None),
    )
    out_specs = (P(("groups", "ctx", "mp"), "rep"), P(("groups", "ctx", "mp"), "rep"))
    return jax.shard_map(
        on_device, mesh=mesh, in_specs=in_specs, out_specs=out_specs, check_vma=False
    )
```

```python
import functools
import math

import jax
import jax.numpy as jnp
from jax import lax
from jax.experimental import pallas as pl
from jax.experimental.pallas import tpu as pltpu
from jax.sharding import PartitionSpec as P

WINDOW = 2048
MESH = pl.DeviceIdType.MESH
F32 = jnp.float32
BF16 = jnp.bfloat16


EARLY_PAIRS = 3


def kernel(
    sizes,
    x_hbm, w_hbm, decay_hbm, q_hbm, kv_hbm,
    att_ref, decay_run, state_run, entering_ref,
    x_ref, wbuf, q_ref, kvbuf, near_top, near_norm, near_out, decay_ref, bias, rate, total, totals_in,
    local_sem, x_send, x_recv, y_send, y_recv, z_send, z_recv, c_send, c_recv,
    e_send, e_recv, k_send, k_recv, r_send, r_recv, t_send, t_recv, near_sem, far_sem,
):
    C, M = sizes
    length = C * M
    rows, width = x_ref.shape
    blocks, depth, bw = wbuf.shape[1], wbuf.shape[3], wbuf.shape[4]
    reach = kvbuf.shape[0] - 1
    hd = kvbuf.shape[3] // 2
    heads = q_ref.shape[1] // hd
    g, c, m, r = (lax.axis_index(n) for n in ("groups", "ctx", "mp", "rep"))
    place = c * M + m
    zb = c % 2
    twin = c + 1 - 2 * zb
    parity = (g + zb) % 2
    corner = 2 * g + zb
    beside_x = lambda d: (g, c, (m + d) % M, r)
    beside_y = (1 - g, c, m, r)
    beside_z = (g, twin, m, r)
    beside_core = (g, c, m, 1 - r)
    below = lambda e: (g, c + e, m, r)

    def at(position):
        return (g, position // M, position % M, r)

    def signal(sem, device):
        pl.semaphore_signal(sem, inc=1, device_id=device, device_id_type=MESH)

    def copy(src, dst, send, recv, device):
        return pltpu.make_async_remote_copy(
            src_ref=src, dst_ref=dst, send_sem=send, recv_sem=recv, device_id=device, device_id_type=MESH
        )

    loads = [
        pltpu.make_async_copy(kv_hbm, kvbuf.at[0, m], local_sem.at[0]),
        pltpu.make_async_copy(x_hbm, x_ref, local_sem.at[1]),
        pltpu.make_async_copy(w_hbm, wbuf.at[:, :, m], local_sem.at[2]),
        pltpu.make_async_copy(q_hbm, q_ref, local_sem.at[3]),
        pltpu.make_async_copy(decay_hbm, decay_ref, local_sem.at[4]),
    ]

    barrier = pltpu.get_barrier_semaphore()
    for d in range(1, M):
        signal(barrier, beside_x(d))

    @pl.when(r == 0)
    def _():
        signal(barrier, beside_core)

    @pl.when(g == 0)
    def _():
        signal(barrier, beside_y)

    @pl.when(c > 0)
    def _():
        signal(barrier, below(-1))

    def greet_later(i, _):
        signal(barrier, at(i))
        return 0

    lax.fori_loop((c + 1) * M, length, greet_later, 0)

    for load in loads:
        load.start()

    def double(par, first, i):
        i = jnp.where(first == 0, i, 5 - i)
        return i % 2, par * 3 + i // 2

    def single(which):
        return which % 2, blocks - 2 + which // 2

    def tile(par, first, which, i):
        return single(which) if i == 0 else double(par, first, i - 1)

    def own(i):
        return tile(parity, g, corner, i)

    def from_y(i):
        return tile(1 - parity, 1 - g, 2 * (1 - g) + zb, i)

    def from_z(i):
        return tile(1 - parity, g, 2 * g + 1 - zb, i)

    def x_copy(d, i, source=0):
        t, b = own(i)
        return copy(w_hbm.at[t, b], wbuf.at[t, b, (m + M - source) % M], x_send.at[d - 1, i], x_recv.at[d - 1, i], beside_x(d))

    def y_copy(d, i, which):
        t, b = which(i)
        piece = wbuf.at[t, b, (m + M - d) % M]
        return copy(piece, piece, y_send.at[d - 1, i], y_recv.at[d - 1, i], beside_y)

    def z_copy(d, i, which):
        t, b = which(i)
        piece = wbuf.at[t, b, (m + M - d) % M]
        return copy(piece, piece, z_send.at[d - 1, i], z_recv.at[d - 1, i], beside_z)

    across = 3 - corner

    def corner_copy(d, which):
        t, b = single(which)
        piece = wbuf.at[t, b, (m + M - d) % M]
        return copy(piece, piece, c_send.at[d - 1], c_recv.at[d - 1], beside_y)

    def relay(i):
        for d in range(1, M):
            x_copy(d, i, d).wait_recv()
            y_copy(d, i, own).start()
            z_copy(d, i, own).start()

    def arrive(i):
        for d in range(1, M):
            x_copy(d, i, d).wait_recv()

    part = rows // 2
    mine = pl.ds(pl.multiple_of(r * part, part), part)
    other = pl.ds(pl.multiple_of((1 - r) * part, part), part)

    def e_copy(d, source=0):
        return copy(kv_hbm.at[mine], kvbuf.at[0, (m + M - source) % M, mine], e_send.at[d - 1], e_recv.at[d - 1], beside_x(d))

    def k_copy(e, d):
        piece = (m + d) % M
        src = kv_hbm.at[mine] if (e, d) == (1, 0) else kvbuf.at[e - 1, piece, mine]
        return copy(src, kvbuf.at[e, piece, mine], k_send.at[e - 1, d], k_recv.at[e - 1, d], below(1))

    def r_copy(i, rows_of):
        piece = kvbuf.at[0, (m + i + 1) % M, rows_of] if i < M - 1 else kvbuf.at[i - M + 2, :, rows_of]
        return copy(piece, piece, r_send.at[i], r_recv.at[i], beside_core)

    pl.semaphore_wait(barrier, M - 1 + g + r + c * M + (c < C - 1).astype(jnp.int32))

    for d in range(1, M):
        x_copy(d, 0).start()
    for d in range(1, M):
        e_copy(d).start()
    for i in range(1, 7):
        for d in range(1, M):
            x_copy(d, i).start()

    @pl.when(r == 1)
    def _():
        signal(near_sem, beside_core)

    @pl.when(g == 1)
    def _():
        signal(near_sem, beside_y)

    def greet(i, _):
        signal(far_sem, at(i))
        return 0

    lax.fori_loop(0, c * M, greet, 0)

    for e in range(1, reach + 1):
        @pl.when(c < e)
        def _(e=e):
            kvbuf[e] = jnp.zeros(kvbuf.shape[1:], BF16)


    @pl.when(c < C - 1)
    def _():
        k_copy(1, 0).start()

    loads[4].wait()
    e = jnp.exp(-decay_ref[...])
    s = e / (2.0 + e)
    s2 = s * s
    rate[...] = -16.0 * s * (1.0 + s2 * (1.0 / 3.0 + s2 * (1.0 / 5.0)))

    row = lax.broadcasted_iota(jnp.int32, (rows, rows), 0)
    col = lax.broadcasted_iota(jnp.int32, (rows, rows), 1)
    for e in range(reach + 1):
        for n in range(M):
            back = row - col + (e * M + m - n) * rows
            allowed = (back >= 0) & (back < WINDOW) & (c >= e)
            first = (e * M + n) * rows
            bias[:, first : first + rows] = jnp.where(allowed, 0.0, -1e30).astype(F32)

    groups8 = rows // 8
    sub = lax.broadcasted_iota(jnp.int32, (groups8, 8, bw), 1)

    def gates(b):
        lanes = pl.ds(pl.multiple_of(b * bw, bw), bw)
        xb = x_ref[:, lanes]
        g0 = jnp.dot(xb, wbuf[0, b].reshape(bw, bw), preferred_element_type=F32)
        g1 = jnp.dot(xb, wbuf[1, b].reshape(bw, bw), preferred_element_type=F32)
        y = rate[:, lanes] * jax.nn.sigmoid(g0)
        poly = 1.0 + y * (1 / 2 + y * (1 / 6 + y * (1 / 24 + y * (1 / 120 + y * (1 / 720)))))
        u = y * poly
        a = (1.0 + u).reshape(groups8, 8, bw)
        v = jnp.sqrt(-u * (2.0 + u)) * jax.nn.sigmoid(g1) * xb.astype(F32)
        v = v.reshape(groups8, 8, bw)
        for shift in (1, 2, 4):
            keep = sub >= shift
            before_v = jnp.where(keep, pltpu.roll(v, shift, 1), 0.0)
            before_a = jnp.where(keep, pltpu.roll(a, shift, 1), 1.0)
            v = a * before_v + v
            a = a * before_a
        ta, tv = jnp.ones((1, bw), F32), jnp.zeros((1, bw), F32)
        for k in range(groups8):
            here = slice(k * 8, k * 8 + 8)
            vk = a[k] * tv + v[k]
            ak = a[k] * ta
            decay_run[here, lanes] = ak
            state_run[here, lanes] = vk
            ta, tv = ak[7:8], vk[7:8]
        return ta, tv

    scale = math.log2(math.e) / math.sqrt(hd)

    def scored(first, last):
        count = (last - first) * M * rows
        q = jnp.concatenate([q_ref[:, h * hd : (h + 1) * hd] for h in range(heads)], axis=0)
        keys = kvbuf[first:last, :, :, :hd].reshape(count, hd)
        scores = lax.dot_general(q, keys, (((1,), (1,)), ((), ())), preferred_element_type=F32)
        scores = scores.reshape(heads, rows, count) * scale + bias[:, first * M * rows : last * M * rows]
        return scores.reshape(heads * rows, count)

    def weighed(weights, first, last):
        values = kvbuf[first:last, :, :, hd:].reshape((last - first) * M * rows, hd)
        return jnp.dot(weights.astype(BF16), values, preferred_element_type=F32)

    def near():
        scores = scored(0, 2)
        top = jnp.max(scores, axis=1, keepdims=True)
        weights = jnp.exp2(scores - top)
        near_top[...] = jnp.broadcast_to(top, near_top.shape)
        near_norm[...] = jnp.broadcast_to(jnp.sum(weights, axis=1, keepdims=True), near_norm.shape)
        near_out[...] = weighed(weights, 0, 2)

    def store(out):
        for h in range(heads):
            att_ref[:, h * hd : (h + 1) * hd] = out[h * rows : (h + 1) * rows].astype(BF16)

    def further(e, last):
        scores = scored(e, e + 1)
        top = jnp.max(scores, axis=1, keepdims=True)
        weights = jnp.exp2(scores - top)
        norm = jnp.broadcast_to(jnp.sum(weights, axis=1, keepdims=True), near_norm.shape)
        top = jnp.broadcast_to(top, near_top.shape)
        both = jnp.maximum(top, near_top[...])
        keep, keep_near = jnp.exp2(top - both), jnp.exp2(near_top[...] - both)
        norm = norm * keep + near_norm[...] * keep_near
        out = weighed(weights, e, e + 1) * keep + near_out[...] * keep_near
        if last:
            store(out / norm)
        else:
            near_top[...] = both
            near_norm[...] = norm
            near_out[...] = out

    ends = jnp.where(g == 0, 0, 2)

    def order(slot):
        mine0, theirs0 = parity * 3, (1 - parity) * 3
        b = theirs0 + 1
        for k, value in enumerate((
            mine0 + ends, blocks - 2 + g, mine0 + 1, theirs0 + 2 - ends, theirs0 + ends, blocks - 1 - g, mine0 + 2 - ends
        )):
            b = jnp.where(slot == k, value, b)
        return b

    def slot_of(b, source_c):
        if b >= blocks - 2:
            return jnp.where(b == blocks - 2 + g, 1, 5)
        par = (g + source_c % 2) % 2
        idx = b % 3
        if idx == 1:
            return jnp.where(par == b // 3, 2, 7)
        same = idx == ends
        return jnp.where(par == b // 3, jnp.where(same, 0, 6), jnp.where(same, 4, 3))

    def t_copy(d, late):
        span = pl.ds(EARLY_PAIRS, blocks // 2 - EARLY_PAIRS) if late else pl.ds(0, EARLY_PAIRS)
        return copy(total.at[span], totals_in.at[d - 1, span], t_send.at[d - 1, late], t_recv.at[d - 1, late], at(place + d))

    def t_start(late):
        def one(d, _):
            t_copy(d, late).start()
            return 0

        lax.fori_loop(1, length - place, one, 0)

    def pass_on(e, ds):
        if e > reach:
            return

        @pl.when(c >= e)
        def _():
            for d in ds:
                k_copy(e, d).wait_recv()

            if e < reach:
                @pl.when(c < C - 1)
                def _():
                    for d in ds:
                        k_copy(e + 1, d).start()

            if ds[-1]:
                r_copy(M - 2 + e, mine).start()

    straight, crossed = (0,), tuple(range(1, M))

    def step(pair, _):
        @pl.when(pair == 0)
        def _():
            pass_on(1, straight)

            @pl.when(g + r < 2)
            def _():
                pl.semaphore_wait(near_sem, 2 - g - r)

            relay(0)
            loads[0].wait()
            for d in range(1, M):
                e_copy(d, d).wait_recv()

            @pl.when(c < C - 1)
            def _():
                for d in range(1, M):
                    k_copy(1, d).start()

            for i in range(M - 1):
                r_copy(i, mine).start()
            pass_on(2, straight)
            relay(1)
            pass_on(1, crossed)
            relay(2)
            for d in range(1, M):
                z_copy(d, 0, from_z).wait_recv()
                corner_copy(d, 2 * g + 1 - zb).start()
            loads[1].wait()
            loads[2].wait()

        @pl.when(pair == 1)
        def _():
            for e in range(3, reach + 1):
                pass_on(e, straight)
            relay(3)
            pass_on(2, crossed)
            loads[3].wait()
            for i in range(M - 1):
                r_copy(i, other).wait_recv()

            @pl.when(c >= 1)
            def _():
                r_copy(M - 1, other).wait_recv()

            near()
            arrive(4)
            for d in range(1, M):
                y_copy(d, 1, from_y).wait_recv()
                y_copy(d, 2, from_y).wait_recv()

        @pl.when(pair == 2)
        def _():
            for d in range(1, M):
                z_copy(d, 1, from_z).wait_recv()
                z_copy(d, 2, from_z).wait_recv()
            for e in range(3, reach + 1):
                pass_on(e, crossed)
            for d in range(1, M):
                y_copy(d, 0, from_y).wait_recv()
                corner_copy(d, across).wait_recv()

        @pl.when(pair == 3)
        def _():
            @pl.when(c < C - 1)
            def _():
                pl.semaphore_wait(far_sem, (C - 1 - c) * M)

            t_start(0)
            arrive(5)
            arrive(6)
            for d in range(1, M):
                y_copy(d, 3, from_y).wait_recv()
                z_copy(d, 3, from_z).wait_recv()

        ends_of = [gates(order(2 * pair + k)) for k in range(2)]
        total[pair] = jnp.concatenate(
            [v[:, q : q + 128] for both in ends_of for v in both for q in (0, 128)], axis=0
        )
        return 0

    lax.fori_loop(0, blocks // 2, step, 0)
    t_start(1)

    for e in range(2, reach + 1):
        @pl.when(c >= e)
        def _(e=e):
            r_copy(M - 2 + e, other).wait_recv()
            further(e, e == reach)

    @pl.when(c < reach)
    def _():
        store(near_out[...] / near_norm[...])

    def t_fold(i, entering):
        d = place - i
        t_copy(d, 0).wait_recv()
        t_copy(d, 1).wait_recv()
        new = []
        for b in range(blocks):
            slot = slot_of(b, i // M)
            first = (slot % 2) * 4
            products = totals_in[d - 1, slot // 2, pl.ds(first, 2)]
            new.append(products * entering[b] + totals_in[d - 1, slot // 2, pl.ds(first + 2, 2)])
        return tuple(new)

    entering = lax.fori_loop(0, place, t_fold, (jnp.zeros((2, 128), F32),) * blocks)
    for b in range(blocks):
        for q in range(2):
            first = b * bw + q * 128
            entering_ref[:, first : first + 128] = entering[b][q : q + 1]

    for d in range(1, M):
        e_copy(d).wait_send()
        for i in range(7):
            x_copy(d, i).wait_send()
        for i in range(4):
            y_copy(d, i, own).wait_send()
            z_copy(d, i, own).wait_send()
        corner_copy(d, 2 * g + 1 - zb).wait_send()
    for i in range(M - 1):
        r_copy(i, mine).wait_send()
    for e in range(1, reach + 1):
        @pl.when(c >= e)
        def _(e=e):
            r_copy(M - 2 + e, mine).wait_send()

    for e in range(1, reach + 1):
        @pl.when((c >= e - 1) & (c < C - 1))
        def _(e=e):
            for d in range(M):
                k_copy(e, d).wait_send()

    def t_sent(d, _):
        t_copy(d, 0).wait_send()
        t_copy(d, 1).wait_send()
        return 0

    lax.fori_loop(1, length - place, t_sent, 0)


PIECES = 4


def finish_kernel(att, decay_run, state_run, entering, rec_out, att_out, rec, sem):
    rows = rec.shape[0]
    step = rows // PIECES
    copies = [pltpu.make_async_copy(att, att_out, sem.at[PIECES])]
    copies[0].start()
    for k in range(PIECES):
        here = pl.ds(k * step, step)
        rec[here] = (state_run[here] + decay_run[here] * entering[...]).astype(BF16)
        copies.append(pltpu.make_async_copy(rec.at[here], rec_out.at[here], sem.at[k]))
        copies[-1].start()
    for copy in copies:
        copy.wait()


def on_device(lru_in, gate_weights, decay_param, queries, keys_values):
    G, C, M, R = (lax.axis_size(n) for n in ("groups", "ctx", "mp", "rep"))
    length = C * M
    rows, width = lru_in.shape
    _, blocks, depth, bw = gate_weights.shape
    assert (G, R, C % 2, blocks, bw) == (2, 2, 0, 8, 256)
    reach = min((WINDOW // rows + M - 1) // M, C - 1)
    hd = keys_values.shape[1] // 2
    stacked = rows * (queries.shape[1] // hd)
    dma = pltpu.SemaphoreType.DMA
    anywhere = pl.BlockSpec(memory_space=pltpu.HBM)
    vmem = pl.BlockSpec(memory_space=pltpu.VMEM)
    parts = pl.pallas_call(
        functools.partial(kernel, (C, M)),
        out_shape=(
            pltpu.VMEM(queries.shape, BF16),
            pltpu.VMEM(lru_in.shape, F32),
            pltpu.VMEM(lru_in.shape, F32),
            pltpu.VMEM((1, width), F32),
        ),
        in_specs=[anywhere] * 5,
        out_specs=(vmem,) * 4,
        scratch_shapes=[
            pltpu.VMEM((rows, width), BF16),
            pltpu.VMEM((2, blocks, M, depth, bw), BF16),
            pltpu.VMEM(queries.shape, BF16),
            pltpu.VMEM((reach + 1, M) + keys_values.shape, BF16),
            pltpu.VMEM((stacked, hd), F32),
            pltpu.VMEM((stacked, hd), F32),
            pltpu.VMEM((stacked, hd), F32),
            pltpu.VMEM((1, width), F32),
            pltpu.VMEM((rows, (reach + 1) * M * rows), F32),
            pltpu.VMEM((1, width), F32),
            pltpu.VMEM((blocks // 2, 8, 128), F32),
            pltpu.VMEM((length - 1, blocks // 2, 8, 128), F32),
            dma((5,)),
            dma((M - 1, 7)),
            dma((M - 1, 7)),
            dma((M - 1, 4)),
            dma((M - 1, 4)),
            dma((M - 1, 4)),
            dma((M - 1, 4)),
            dma((M - 1,)),
            dma((M - 1,)),
            dma((M - 1,)),
            dma((M - 1,)),
            dma((reach, M)),
            dma((reach, M)),
            dma((reach + M - 1,)),
            dma((reach + M - 1,)),
            dma((length - 1, 2)),
            dma((length - 1, 2)),
            pltpu.SemaphoreType.REGULAR,
            pltpu.SemaphoreType.REGULAR,
        ],
        compiler_params=pltpu.CompilerParams(
            collective_id=0, has_side_effects=True, vmem_limit_bytes=64 * 2**20 - 917504 - 2440000
        ),
    )(lru_in, gate_weights, decay_param.reshape(1, width), queries, keys_values)
    return pl.pallas_call(
        finish_kernel,
        out_shape=(
            jax.ShapeDtypeStruct(lru_in.shape, BF16),
            jax.ShapeDtypeStruct(queries.shape, BF16),
        ),
        in_specs=[vmem] * 4,
        out_specs=(anywhere, anywhere),
        scratch_shapes=[pltpu.VMEM((rows, width), BF16), dma((PIECES + 1,))],
        compiler_params=pltpu.CompilerParams(vmem_limit_bytes=8 * 2**20),
    )(*parts)


def solution(mesh):
    in_specs = (
        P(("groups", "ctx", "mp"), "rep"),
        P(None, "rep", "mp", None),
        P("rep"),
        P(("groups", "ctx", "mp"), "rep"),
        P(("groups", "ctx", "mp"), None),
    )
    out_specs = (P(("groups", "ctx", "mp"), "rep"), P(("groups", "ctx", "mp"), "rep"))
    return jax.shard_map(
        on_device, mesh=mesh, in_specs=in_specs, out_specs=out_specs, check_vma=False
    )
```
